256 devices in a mesh: row: 8 (over x, core), col: 32 (over z, y).
Axes of the slice: x: 4, y: 4, z: 8, core: 2. Of those that a mesh axis runs over, the one named last changes fastest.
Arguments:
- slab_pos: bfloat16 [64, 16384], P(None, ('row', 'col')), may hold values from -1 to 1
- slab_bias: bfloat16 [16384], P(('row', 'col')), may hold values from -1.5 to 1.5
- node_pos: bfloat16 [64, 262144], P(None, ('col', 'row')), may hold values from -1 to 1
- node_bias: bfloat16 [262144], P(('col', 'row')), may hold values from -1.5 to 1.5
- alpha: float32 [], replicated, may hold values from 6 to 7
- edge_counts: int32 [4096, 128, 128], P(('row', 'col')), may hold values from 0 to 99
- edge_blocks: int32 [4096, 2], P(('row', 'col')), may hold values from 0 to 63, as said below
Outputs:
- slab_pos_grad: float32 [64, 16384], P(None, ('row', 'col'))
- slab_bias_grad: float32 [16384], P(('row', 'col'))
- node_pos_grad: float32 [64, 262144], P(None, ('col', 'row'))
- node_bias_grad: float32 [262144], P(('col', 'row'))
The draws below stay inside these ranges and needn't reach their ends.
Inputs may be any that keep to these rules, and one draw needn't show every extreme that they name: `edge_blocks`: within the 16 rows of one block pair (rows b * 16 to b * 16 + 15) no pair (row block, column block) repeats; the row block is below 16 and the column block below 64.
All inputs are finite; a program needn't handle non-finite values.
Results may differ from the reference program's by a relative error of at most 0.004.
Values may be sent and summed in bfloat16 or wider, within the bound.
A program may use at most 64 MiB of HBM per device.

```python
import jax
import jax.numpy as jnp
from jax import lax

D = 64
TB = 128
ROWS_TILE = 2048
COLS_TILE = 8192
K_TILES = 16
SLAB = 16384
NODES = 262144
TILES = 4096
N_COL = 32


def draw_edge_blocks(key, part):
    groups = TILES // K_TILES
    col_tiles = COLS_TILE // TB
    places = ROWS_TILE // TB * col_tiles
    keys = jax.random.split(jax.random.fold_in(key, 17), groups)
    picks = jax.vmap(lambda one_key: jax.random.permutation(one_key, places)[:K_TILES])(keys)
    first_key = jax.random.fold_in(key, 29)
    first_rest = jax.random.permutation(first_key, places - 1)[:K_TILES - 1]
    first_group = jnp.concatenate([jnp.array([places - 1], dtype=jnp.int32), first_rest.astype(jnp.int32)])
    picks = picks.astype(jnp.int32).at[0].set(first_group)
    row_block = picks // col_tiles
    col_block = picks % col_tiles
    return jnp.stack([row_block, col_block], axis=-1).reshape(TILES, 2).astype(jnp.int32)


def touch_ends(result, key, low, high):
    index_at = [jax.random.randint(jax.random.fold_in(key, axis), (), 0, length) for axis, length in enumerate(result.shape)]
    longest = result.shape.index(max(result.shape))
    beside = index_at[:longest] + [(index_at[longest] + 1) % result.shape[longest]] + index_at[longest + 1:]
    return result.at[tuple(index_at)].set(low).at[tuple(beside)].set(high)


def level_of(stream_key, shape, shards, low, largest):
    level = 1.0
    for axis_at, shards_of in shards:
        draws = jax.random.uniform(jax.random.fold_in(jax.random.fold_in(stream_key, 6), axis_at), (shards_of,), jnp.float32, low / len(shards), largest / len(shards))
        level = level * jnp.repeat(jnp.exp(draws), shape[axis_at] // shards_of).reshape((-1,) + (1,) * (len(shape) - 1 - axis_at))
    return level


def bell_draw(own_key, shape, width, bound, pieces=(), kind=jnp.bfloat16):
    values = jax.random.normal(own_key, shape, jnp.float32) * width
    if len(pieces) > 0:
        values = level_of(own_key, shape, pieces, -0.22, 0.18) * values
    return jnp.clip(values, min=-bound, max=bound).astype(kind)


def setup_inputs(seed: int = 0) -> dict:
    seeds = jax.random.split(jax.random.key(seed), 8)
    return {
        "slab_pos": bell_draw(seeds[0], (D, SLAB), 0.25, 1.0, ((1, 256),)),
        "slab_bias": bell_draw(seeds[1], (SLAB,), 0.5, 1.5, ((0, 256),)),
        "node_pos": bell_draw(seeds[2], (D, NODES), 0.25, 1.0, ((1, 256),)),
        "node_bias": bell_draw(seeds[3], (NODES,), 0.5, 1.5, ((0, 256),)),
        "alpha": jnp.clip(jax.random.uniform(seeds[4], (), jnp.float32, 6.0, 7.0), 6.0, 7.0),
        "edge_counts": touch_ends(jax.random.randint(seeds[5], (TILES, TB, TB), 0, 100), jax.random.fold_in(seeds[5], 1), 0, 99).astype(jnp.int32),
        "edge_blocks": draw_edge_blocks(jax.random.fold_in(seeds[7], 71), 0),
    }


def rates(row_pos, row_bias, col_pos, col_bias, alpha):
    rowf = row_pos.astype(jnp.float32)
    colf = col_pos.astype(jnp.float32)
    row_norm = jnp.sum(rowf * rowf, axis=0)
    col_norm = jnp.sum(colf * colf, axis=0)
    cross = lax.dot_general(row_pos, col_pos, (((0,), (0,)), ((), ())), preferred_element_type=jnp.float32)
    dist = row_norm[:, None] + col_norm[None, :] - 2.0 * cross
    eta = alpha + row_bias.astype(jnp.float32)[:, None] + col_bias.astype(jnp.float32)[None, :] - dist
    return jnp.exp(eta).astype(jnp.bfloat16)


def reference(slab_pos, slab_bias, node_pos, node_bias, alpha, edge_counts, edge_blocks):
    n_rb = SLAB // ROWS_TILE
    n_cb = NODES // COLS_TILE
    slab_stack = slab_pos.reshape(D, n_rb, ROWS_TILE).transpose(1, 0, 2)
    slab_bstack = slab_bias.reshape(n_rb, ROWS_TILE)
    node_stack = node_pos.reshape(D, n_cb, COLS_TILE).transpose(1, 0, 2)
    node_bstack = node_bias.reshape(n_cb, COLS_TILE)

    def outer(col_carry, xs):
        row_blk, row_b = xs

        def inner(row_carry, ys):
            col_blk, col_b = ys
            lam = rates(row_blk, row_b, col_blk, col_b, alpha)
            lamf = lam.astype(jnp.float32)
            racc = jnp.dot(col_blk, lam.T, preferred_element_type=jnp.float32)
            cacc = jnp.dot(row_blk, lam, preferred_element_type=jnp.float32)
            return (row_carry[0] + racc, row_carry[1] + jnp.sum(lamf, axis=1)), (cacc, jnp.sum(lamf, axis=0))

        init = (jnp.zeros((D, ROWS_TILE), jnp.float32), jnp.zeros((ROWS_TILE,), jnp.float32))
        (racc, rtot), (caccs, ctots) = lax.scan(inner, init, (node_stack, node_bstack))
        cacc = caccs.transpose(1, 0, 2).reshape(D, NODES)
        ctot = ctots.reshape(NODES)
        return (col_carry[0] + cacc, col_carry[1] + ctot), (racc, rtot)

    cinit = (jnp.zeros((D, NODES), jnp.float32), jnp.zeros((NODES,), jnp.float32))
    (rate_cacc, rate_ctot), (raccs, rtots) = lax.scan(outer, cinit, (slab_stack, slab_bstack))
    rate_racc = raccs.transpose(1, 0, 2).reshape(D, SLAB)
    rate_rtot = rtots.reshape(SLAB)

    n_rt = ROWS_TILE // TB
    n_ct = COLS_TILE // TB
    device = jnp.arange(TILES, dtype=jnp.int32) // K_TILES
    grow = (device // N_COL) * n_rt + edge_blocks[:, 0]
    gcol = (device % N_COL) * n_ct + edge_blocks[:, 1]
    slab_tiles = jnp.take(slab_pos.reshape(D, SLAB // TB, TB).astype(jnp.float32), grow, axis=1)
    node_tiles = jnp.take(node_pos.reshape(D, NODES // TB, TB).astype(jnp.float32), gcol, axis=1)
    counts = edge_counts.astype(jnp.float32)
    hi = lax.Precision.HIGHEST
    redge = jnp.einsum('dkj,kij->dki', node_tiles, counts, precision=hi)
    cedge = jnp.einsum('dki,kij->dkj', slab_tiles, counts, precision=hi)
    rtot_e = jnp.sum(counts, axis=2)
    ctot_e = jnp.sum(counts, axis=1)
    row_edge = jnp.zeros((D, SLAB // TB, TB), jnp.float32).at[:, grow, :].add(redge).reshape(D, SLAB)
    row_edge_tot = jnp.zeros((SLAB // TB, TB), jnp.float32).at[grow, :].add(rtot_e).reshape(SLAB)
    col_edge = jnp.zeros((D, NODES // TB, TB), jnp.float32).at[:, gcol, :].add(cedge).reshape(D, NODES)
    col_edge_tot = jnp.zeros((NODES // TB, TB), jnp.float32).at[gcol, :].add(ctot_e).reshape(NODES)

    row_acc = row_edge - rate_racc
    row_tot = row_edge_tot - rate_rtot
    col_acc = col_edge - rate_cacc
    col_tot = col_edge_tot - rate_ctot
    slab_f = slab_pos.astype(jnp.float32)
    node_f = node_pos.astype(jnp.float32)
    slab_pos_grad = -2.0 * (slab_f * row_tot[None, :] - row_acc) / NODES
    slab_bias_grad = row_tot / NODES
    node_pos_grad = 2.0 * (col_acc - node_f * col_tot[None, :]) / SLAB
    node_bias_grad = col_tot / SLAB
    return (slab_pos_grad, slab_bias_grad, node_pos_grad, node_bias_grad)
```

```python
import functools

import jax
import jax.numpy as jnp
from jax import lax
from jax.experimental import pallas as pl
from jax.experimental.pallas import tpu as pltpu
from jax.sharding import PartitionSpec as P

MESH = pl.DeviceIdType.MESH
F32 = jnp.float32
BF16 = jnp.bfloat16
LOG2E = 1.4426950408889634
NX, NY, NZ = 4, 4, 8
XD = YD = (1, 3, 2)
ZD = (1, 7, 2, 6, 3, 5, 4)
PB, QB = 512, 1024
KROWS = 80
OROWS = 72
VMEM_LIMIT = 52 * 1024 * 1024


def split3(v):
    a = v.astype(BF16).astype(F32)
    b = (v - a).astype(BF16).astype(F32)
    c = (v - a - b).astype(BF16).astype(F32)
    return a, b, c


def extras(scalars):
    a, b, c = split3(scalars)
    i = lax.broadcasted_iota(jnp.int32, (16, scalars.shape[1]), 0)
    one = jnp.where((i == 0) | (i == 4) | (i == 5), 1.0, 0.0)
    ext = jnp.where(i == 1, a, jnp.where(i == 2, b, jnp.where(i == 3, c, one)))
    return ext.astype(BF16)


def position():
    row, col = lax.axis_index("row"), lax.axis_index("col")
    return row // 2, row % 2, col % NY, col // NY


def enter(peers):
    barrier = pltpu.get_barrier_semaphore()
    for peer in peers:
        pl.semaphore_signal(barrier, inc=1, device_id=peer, device_id_type=MESH)
    pl.semaphore_wait(barrier, len(peers))


def all_peers():
    x, core, y, z = position()
    row, col = lax.axis_index("row"), lax.axis_index("col")
    xs = {d: {"row": (x + d) % NX * 2 + core, "col": col} for d in XD}
    sibling = {"row": x * 2 + 1 - core, "col": col}
    ys = {d: {"row": row, "col": z * NY + (y + d) % NY} for d in YD}
    zs = {d: {"row": row, "col": (z + d) % NZ * NY + y} for d in ZD}
    return xs, sibling, ys, zs


def remote(src, dst, ssem, rsem, peer):
    return pltpu.make_async_remote_copy(
        src_ref=src, dst_ref=dst, send_sem=ssem, recv_sem=rsem, device_id=peer, device_id_type=MESH
    )


def columns(ref, index, width):
    return ref.at[:, pl.ds(pl.multiple_of(index * width, 128), width)]


def gather_kernel(
    alpha_ref, spos_ref, sbias_ref, npos_ref, nbias_ref, s_ref, n_ref,
    ypiece, n_send, n_recv, f_send, f_recv, y_send, y_recv, z_send, z_recv,
):
    x, core, y, z = position()
    xs, sibling, ys, zs = all_peers()
    width = npos_ref.shape[1]
    enter([xs[d] for d in XD] + [sibling] + [ys[d] for d in YD] + [zs[d] for d in ZD])

    sp = spos_ref[...].astype(F32)
    u = LOG2E * (alpha_ref[0, 0] + sbias_ref[...].astype(F32) - jnp.sum(sp * sp, axis=0, keepdims=True))
    ypiece[y] = jnp.zeros((KROWS, 128), BF16)
    ypiece[y, 0:64, 0:64] = spos_ref[...]
    ypiece[y, 64:80, 0:64] = extras(u)
    ycopies = {d: remote(ypiece.at[y], ypiece.at[y], y_send.at[d], y_recv.at[d], ys[d]) for d in YD}
    for d in YD:
        ycopies[d].start()

    nodes = npos_ref[...].astype(F32)
    v = LOG2E * (nbias_ref[...].astype(F32) - jnp.sum(nodes * nodes, axis=0, keepdims=True))
    mine = columns(n_ref, x * 2 + core, width)
    mine[0:64, :] = npos_ref[...]
    mine[64:80, :] = extras(v)
    ncopies = {d: remote(mine, mine, n_send.at[d], n_recv.at[d], xs[d]) for d in XD}
    for d in XD:
        ncopies[d].start()
    fcopies = {0: remote(mine, mine, f_send.at[0], f_recv.at[0], sibling)}
    fcopies[0].start()

    for d in YD:
        ycopies[d].wait_recv()
    lane = lax.broadcasted_iota(jnp.int32, (KROWS, 128), 1)
    zv = columns(s_ref, z, 256)
    for h in range(2):
        a, b = ypiece[2 * h].astype(F32), ypiece[2 * h + 1].astype(F32)
        zv[:, h * 128 : h * 128 + 128] = jnp.where(lane < 64, a, pltpu.roll(b, 64, 1)).astype(BF16)
    zcopies = {d: remote(zv, zv, z_send.at[d], z_recv.at[d], zs[d]) for d in ZD}
    for d in ZD:
        zcopies[d].start()

    for d in XD:
        ncopies[d].wait_recv()
        piece = columns(n_ref, (x + NX - d) % NX * 2 + core, width)
        fcopies[d] = remote(piece, piece, f_send.at[d], f_recv.at[d], sibling)
        fcopies[d].start()
    for group in (fcopies, zcopies):
        for d in group:
            group[d].wait_recv()
    for group in (ycopies, ncopies, fcopies, zcopies):
        for d in group:
            group[d].wait_send()


def local_kernel(blocks_ref, counts_ref, s_ref, n_ref, r_ref, c_ref, a_ref, nt_ref, racc):
    rows, cols = s_ref.shape[1], n_ref.shape[1]
    for i in range(rows // 256):
        sl = pl.ds(i * 256, 256)
        s = s_ref[:, sl].astype(F32)
        h1, h2, h3 = split3(s[0:64] * (2.0 * LOG2E))
        k = lax.broadcasted_iota(jnp.int32, (16, 256), 0)
        one = jnp.where((k >= 1) & (k <= 3), 1.0, 0.0)
        e = jnp.where(k == 0, s[65:66], jnp.where(k == 4, s[66:67], jnp.where(k == 5, s[67:68], one)))
        t = jnp.concatenate([h1, h2, h3, e, jnp.zeros((48, 256), F32)], axis=0)
        a_ref[sl, :] = t.T.astype(BF16)
    racc[...] = jnp.zeros_like(racc)

    def chunk(j, _):
        q = pl.ds(pl.multiple_of(j * QB, 128), QB)
        n = n_ref[:, q]
        b = jnp.concatenate([n[0:64], n[0:64], n, jnp.zeros((48, QB), BF16)], axis=0)
        nt = jnp.concatenate([n.astype(F32), jnp.zeros((48, QB), F32)], axis=0).T.astype(BF16)
        nt_ref[q, :] = nt
        cacc = jnp.zeros((KROWS, QB), F32)
        for i in range(rows // PB):
            sl = pl.ds(i * PB, PB)
            t = jnp.dot(a_ref[sl, :], b, preferred_element_type=F32)
            lam = jnp.exp2(t).astype(BF16)
            racc[sl, :] -= jnp.dot(lam, nt, preferred_element_type=F32)
            cacc += jnp.dot(s_ref[:, sl], lam, preferred_element_type=F32)
        c_ref[:, q] = -cacc[0:OROWS]
        return 0

    lax.fori_loop(0, cols // QB, chunk, 0)

    def edge(k, _):
        p = pl.ds(pl.multiple_of(blocks_ref[k, 0] * 128, 128), 128)
        q = pl.ds(pl.multiple_of(blocks_ref[k, 1] * 128, 128), 128)
        y = counts_ref[k].astype(F32).astype(BF16)
        racc[p, :] += jnp.dot(y, nt_ref[q, :], preferred_element_type=F32)
        c_ref[:, q] += jnp.dot(s_ref[:, p], y, preferred_element_type=F32)[0:OROWS]
        return 0

    lax.fori_loop(0, counts_ref.shape[0], edge, 0)
    for i in range(rows // 256):
        sl = pl.ds(i * 256, 256)
        r_ref[:, sl] = racc[sl, :].T[0:OROWS]


def scatter_kernel(
    spos_ref, npos_ref, r_ref, c_ref, sg_ref, sb_ref, ng_ref, nb_ref,
    sib, xbuf, xin, zin, yblk, yin, f_send, f_recv, x_send, x_recv, z_send, z_recv, y_send, y_recv,
    *, n_nodes, n_slab,
):
    x, core, y, z = position()
    xs, sibling, ys, zs = all_peers()
    width = npos_ref.shape[1]
    enter([xs[d] for d in XD] + [sibling] + [ys[d] for d in YD] + [zs[d] for d in ZD])

    zcopies = {}
    for d in ZD:
        zcopies[d] = remote(columns(r_ref, (z + d) % NZ, 256), zin.at[d], z_send.at[d], z_recv.at[d], zs[d])
        zcopies[d].start()
    scopies, xcopies = {}, {}
    for d in XD + (0,):
        src = columns(c_ref, (x + d) % NX * 2 + 1 - core, width)
        scopies[d] = remote(src, sib.at[d], f_send.at[d], f_recv.at[d], sibling)
        scopies[d].start()
    for d in XD:
        scopies[d].wait_recv()
        xbuf[d] = columns(c_ref, (x + d) % NX * 2 + core, width)[...] + sib[d]
        xcopies[d] = remote(xbuf.at[d], xin.at[d], x_send.at[d], x_recv.at[d], xs[d])
        xcopies[d].start()

    for d in ZD:
        zcopies[d].wait_recv()
    total = columns(r_ref, z, 256)[...]
    for d in ZD:
        total += zin[d]
    yblk[0] = total[:, 0:128]
    yblk[1] = total[:, 128:256]
    ycopies = {}
    for d in YD:
        ycopies[d] = remote(yblk.at[(y + d) % NY // 2], yin.at[d], y_send.at[d], y_recv.at[d], ys[d])
        ycopies[d].start()
    for d in YD:
        ycopies[d].wait_recv()
    mine = yblk[y // 2]
    for d in YD:
        mine += yin[d]
    odd = jnp.broadcast_to(y % 2, mine.shape) == 1
    mine = jnp.where(odd, pltpu.roll(mine, 64, 1), mine)[:, 0:64]
    tot = mine[64:65]
    sg_ref[...] = (spos_ref[...].astype(F32) * tot - mine[0:64]) * (-2.0 / n_nodes)
    sb_ref[...] = tot * (1.0 / n_nodes)

    scopies[0].wait_recv()
    for d in XD:
        xcopies[d].wait_recv()
    for h in range(width // 256):
        sl = pl.ds(h * 256, 256)
        acc = columns(c_ref, x * 2 + core, width)[:, sl] + sib[0, :, sl]
        for d in XD:
            acc += xin[d, :, sl]
        tot = acc[64:65]
        ng_ref[:, sl] = (acc[0:64] - npos_ref[:, sl].astype(F32) * tot) * (2.0 / n_slab)
        nb_ref[:, sl] = tot * (1.0 / n_slab)
    for group in (zcopies, scopies, xcopies, ycopies):
        for d in group:
            group[d].wait_send()


def params(**kw):
    return pltpu.CompilerParams(vmem_limit_bytes=VMEM_LIMIT, **kw)


def local(slab_pos, slab_bias, node_pos, node_bias, alpha, edge_counts, edge_blocks):
    vmem = pl.BlockSpec(memory_space=pltpu.VMEM)
    smem = pl.BlockSpec(memory_space=pltpu.SMEM)
    dma = pltpu.SemaphoreType.DMA
    own_rows, own_cols = slab_pos.shape[1], node_pos.shape[1]
    rows = own_rows * lax.axis_size("col")
    cols = own_cols * lax.axis_size("row")
    n_slab = rows * lax.axis_size("row")
    n_nodes = cols * lax.axis_size("col")
    slab, nodes = pl.pallas_call(
        gather_kernel,
        out_shape=(jax.ShapeDtypeStruct((KROWS, rows), BF16), jax.ShapeDtypeStruct((KROWS, cols), BF16)),
        in_specs=[smem, vmem, vmem, vmem, vmem],
        out_specs=(vmem, vmem),
        scratch_shapes=[pltpu.VMEM((NY, KROWS, 128), BF16)]
        + [dma((NX,))] * 4 + [dma((NY,))] * 2 + [dma((NZ,))] * 2,
        compiler_params=params(collective_id=0, has_side_effects=True),
        name="gather",
    )(alpha.reshape(1, 1), slab_pos, slab_bias.reshape(1, own_rows), node_pos, node_bias.reshape(1, own_cols))
    row_sums, col_sums = pl.pallas_call(
        local_kernel,
        out_shape=(jax.ShapeDtypeStruct((OROWS, rows), F32), jax.ShapeDtypeStruct((OROWS, cols), F32)),
        in_specs=[smem, vmem, vmem, vmem],
        out_specs=(vmem, vmem),
        scratch_shapes=[
            pltpu.VMEM((rows, 256), BF16), pltpu.VMEM((cols, 128), BF16), pltpu.VMEM((rows, 128), F32),
        ],
        compiler_params=params(),
        name="sweep",
    )(edge_blocks, edge_counts, slab, nodes)
    piece = pltpu.VMEM((NX, OROWS, own_cols), F32)
    sg, sb, ng, nb = pl.pallas_call(
        functools.partial(scatter_kernel, n_nodes=n_nodes, n_slab=n_slab),
        out_shape=(
            jax.ShapeDtypeStruct((64, own_rows), F32), jax.ShapeDtypeStruct((1, own_rows), F32),
            jax.ShapeDtypeStruct((64, own_cols), F32), jax.ShapeDtypeStruct((1, own_cols), F32),
        ),
        in_specs=[vmem] * 4,
        out_specs=(vmem,) * 4,
        scratch_shapes=[
            piece, piece, piece, pltpu.VMEM((NZ, OROWS, 256), F32),
            pltpu.VMEM((2, OROWS, 128), F32), pltpu.VMEM((NY, OROWS, 128), F32),
        ] + [dma((NX,))] * 4 + [dma((NZ,))] * 2 + [dma((NY,))] * 2,
        compiler_params=params(collective_id=1, has_side_effects=True),
        name="scatter",
    )(slab_pos, node_pos, row_sums, col_sums)
    return sg, sb.reshape(own_rows), ng, nb.reshape(own_cols)


def solution(mesh):
    in_specs = (
        P(None, ("row", "col")),
        P(("row", "col")),
        P(None, ("col", "row")),
        P(("col", "row")),
        P(),
        P(("row", "col"), None, None),
        P(("row", "col"), None),
    )
    out_specs = (
        P(None, ("row", "col")),
        P(("row", "col")),
        P(None, ("col", "row")),
        P(("col", "row")),
    )
    return jax.shard_map(local, mesh=mesh, in_specs=in_specs, out_specs=out_specs, check_vma=False)
```

```python
import functools

import jax
import jax.numpy as jnp
from jax import lax
from jax.experimental import pallas as pl
from jax.experimental.pallas import tpu as pltpu
from jax.sharding import PartitionSpec as P

MESH = pl.DeviceIdType.MESH
F32 = jnp.float32
BF16 = jnp.bfloat16
LOG2E = 1.4426950408889634
NX, NY, NZ = 4, 4, 8
XD = YD = (1, 3, 2)
ZD = (1, 7, 2, 6, 3, 5, 4)
ORDER = (4, 3, 5, 2, 6, 7, 1, 0)
SLOT = {d: s for s, d in enumerate(ORDER)}
PB, QB = 512, 1024
TB = 128
KROWS = 80
OROWS = 72
VMEM_LIMIT = 52 * 1024 * 1024


def split3(v):
    a = v.astype(BF16).astype(F32)
    b = (v - a).astype(BF16).astype(F32)
    c = (v - a - b).astype(BF16).astype(F32)
    return a, b, c


def extras(scalars):
    a, b, c = split3(scalars)
    i = lax.broadcasted_iota(jnp.int32, (16, scalars.shape[1]), 0)
    one = jnp.where((i == 0) | (i == 4) | (i == 5), 1.0, 0.0)
    ext = jnp.where(i == 1, a, jnp.where(i == 2, b, jnp.where(i == 3, c, one)))
    return ext.astype(BF16)


def position():
    row, col = lax.axis_index("row"), lax.axis_index("col")
    return row // 2, row % 2, col % NY, col // NY


def enter(peers):
    barrier = pltpu.get_barrier_semaphore()
    for peer in peers:
        pl.semaphore_signal(barrier, inc=1, device_id=peer, device_id_type=MESH)
    pl.semaphore_wait(barrier, len(peers))


def all_peers():
    x, core, y, z = position()
    row, col = lax.axis_index("row"), lax.axis_index("col")
    xs = {d: {"row": (x + d) % NX * 2 + core, "col": col} for d in XD}
    sibling = {"row": x * 2 + 1 - core, "col": col}
    ys = {d: {"row": row, "col": z * NY + (y + d) % NY} for d in YD}
    zs = {d: {"row": row, "col": (z + d) % NZ * NY + y} for d in ZD}
    return xs, sibling, ys, zs


def remote(src, dst, ssem, rsem, peer):
    return pltpu.make_async_remote_copy(
        src_ref=src, dst_ref=dst, send_sem=ssem, recv_sem=rsem, device_id=peer, device_id_type=MESH
    )


def columns(ref, index, width):
    return ref.at[:, pl.ds(pl.multiple_of(index * width, 128), width)]


def params(**kw):
    return pltpu.CompilerParams(vmem_limit_bytes=VMEM_LIMIT, **kw)


def body(
    blocks_ref, alpha_ref, sbias_ref, nbias_ref, spos_hbm, npos_hbm, counts_hbm,
    sg_ref, sb_ref, ng_ref, nb_ref,
    spos_ref, npos_ref, counts_ref, in_sem,
    s_ref, n_ref, nt_ref, st_ref, a_ref, racc, cacc, erow, ecol,
    ypiece, sib, xbuf, xin, zout, zin, yblk, yin,
    n_send, n_recv, f_send, f_recv, y_send, y_recv, z_send, z_recv,
    cf_send, cf_recv, cx_send, cx_recv, rz_send, rz_recv, ry_send, ry_recv,
    *, n_nodes, n_slab,
):
    x, core, y, z = position()
    xs, sibling, ys, zs = all_peers()
    width = npos_ref.shape[1]
    tiles = counts_ref.shape[0]
    copies = []

    def send(src, dst, ssem, rsem, peer):
        c = remote(src, dst, ssem, rsem, peer)
        c.start()
        copies.append(c)
        return c

    loads = [
        pltpu.make_async_copy(a, b, in_sem.at[i])
        for i, (a, b) in enumerate(((spos_hbm, spos_ref), (npos_hbm, npos_ref), (counts_hbm, counts_ref)))
    ]
    for c in loads:
        c.start()
    enter([xs[d] for d in XD] + [sibling] + [ys[d] for d in YD] + [zs[d] for d in ZD])

    loads[0].wait()
    sp = spos_ref[...].astype(F32)
    u = LOG2E * (alpha_ref[0, 0] + sbias_ref[...].astype(F32) - jnp.sum(sp * sp, axis=0, keepdims=True))
    ypiece[y] = jnp.zeros((KROWS, 128), BF16)
    ypiece[y, 0:64, 0:64] = spos_ref[...]
    ypiece[y, 64:80, 0:64] = extras(u)
    yget = {d: send(ypiece.at[y], ypiece.at[y], y_send.at[d], y_recv.at[d], ys[d]) for d in YD}

    loads[1].wait()
    nodes = npos_ref[...].astype(F32)
    nb = nbias_ref[...].astype(F32)
    nb = jnp.concatenate([nb[i : i + 1] for i in range(width // 128)], axis=1)
    v = LOG2E * (nb - jnp.sum(nodes * nodes, axis=0, keepdims=True))
    mine = columns(n_ref, x * 2 + core, width)
    mine[0:64, :] = npos_ref[...]
    mine[64:80, :] = extras(v)
    nget = {d: send(mine, mine, n_send.at[d], n_recv.at[d], xs[d]) for d in XD}
    f0 = send(mine, mine, f_send.at[0], f_recv.at[0], sibling)

    racc[...] = jnp.zeros_like(racc)
    cacc[...] = jnp.zeros_like(cacc)

    for d in YD:
        yget[d].wait_recv()
    lane = lax.broadcasted_iota(jnp.int32, (KROWS, 128), 1)
    own = s_ref.at[:, pl.ds(SLOT[0] * 256, 256)]
    for h in range(2):
        a, b = ypiece[2 * h].astype(F32), ypiece[2 * h + 1].astype(F32)
        own[:, h * 128 : h * 128 + 128] = jnp.where(lane < 64, a, pltpu.roll(b, 64, 1)).astype(BF16)
    zget = {}
    for d in ORDER[:-1]:
        dst = s_ref.at[:, pl.ds(SLOT[d] * 256, 256)]
        zget[d] = send(own, dst, z_send.at[d], z_recv.at[d], zs[d])

    def prep_rows(slot):
        sl = pl.ds(slot * 256, 256)
        s = s_ref[:, sl].astype(F32)
        h1, h2, h3 = split3(s[0:64] * (2.0 * LOG2E))
        k = lax.broadcasted_iota(jnp.int32, (16, 256), 0)
        one = jnp.where((k >= 1) & (k <= 3), 1.0, 0.0)
        e = jnp.where(k == 0, s[65:66], jnp.where(k == 4, s[66:67], jnp.where(k == 5, s[67:68], one)))
        t = jnp.concatenate([h1, h2, h3, e, jnp.zeros((48, 256), F32)], axis=0)
        a_ref[sl, :] = t.T.astype(BF16)

    def chunk(j):
        return pl.ds(pl.multiple_of(j * QB, QB), QB)

    def prep_cols(j):
        n = n_ref[:, chunk(j)]
        t = jnp.concatenate([n.astype(F32), jnp.zeros((48, QB), F32)], axis=0).T.astype(BF16)
        nt_ref[pl.ds(j * (QB // TB), QB // TB)] = t.reshape(QB // TB, TB, 128)

    def unit(pair, j):
        q = chunk(j)
        sl = pl.ds(pl.multiple_of(pair * PB, PB), PB)
        n = n_ref[:, q]
        b = jnp.concatenate([n[0:64], n[0:64], n, jnp.zeros((48, QB), BF16)], axis=0)
        t = jnp.dot(a_ref[sl, :], b, preferred_element_type=F32)
        lam = jnp.exp2(t).astype(BF16)
        racc[sl, :] -= jnp.dot(
            lam, nt_ref[pl.ds(j * (QB // TB), QB // TB)].reshape(QB, 128), preferred_element_type=F32
        )
        cacc[:, q] -= jnp.dot(s_ref[:, sl], lam, preferred_element_type=F32)[0:OROWS]

    def spans(n, f):
        def step(i, _):
            f(i)
            return 0

        lax.fori_loop(0, n, step, 0)

    def chip(d):
        return (x + d) % NX

    for d in ORDER[0:2]:
        zget[d].wait_recv()
        prep_rows(SLOT[d])

    def first_own(i):
        j = x * 2 + (core + i) % 2

        @pl.when(i == 1)
        def _():
            f0.wait_recv()

        prep_cols(j)
        unit(0, j)

    spans(2, first_own)

    def first_others(i):
        d = 1 + i // 2
        src = chip(NX - d)
        h = i % 2

        @pl.when(h == 0)
        def _():
            piece = columns(n_ref, src * 2 + core, width)
            remote(piece, piece, n_send.at[d], n_recv.at[d], sibling).wait_recv()
            remote(piece, piece, f_send.at[d], f_recv.at[d], sibling).start()

        @pl.when(h == 1)
        def _():
            piece = columns(n_ref, src * 2 + 1 - core, width)
            remote(piece, piece, f_send.at[d], f_recv.at[d], sibling).wait_recv()

        j = src * 2 + (core + h) % 2
        prep_cols(j)
        unit(0, j)

    spans(6, first_others)
    for d in XD:
        piece = columns(n_ref, chip(NX - d) * 2 + core, width)
        copies.append(remote(piece, piece, f_send.at[d], f_recv.at[d], sibling))

    for d in ORDER[2:-1]:
        zget[d].wait_recv()
    for d in ORDER[2:]:
        prep_rows(SLOT[d])

    loads[2].wait()

    for d in ORDER:
        for h in range(2):
            st_ref[(z + NZ - d) % NZ * 2 + h] = s_ref[:, pl.ds(SLOT[d] * 256 + h * TB, TB)]

    def edge(k):
        yk = counts_ref[k].astype(F32).astype(BF16)
        erow[k] = jnp.dot(yk, nt_ref[blocks_ref[1, k]], preferred_element_type=F32)
        ecol[k] = jnp.dot(st_ref[blocks_ref[0, k]], yk, preferred_element_type=F32)[0:OROWS]

    def same(a, b):
        return (1 - jnp.minimum((a - b) * (a - b), 1)).astype(F32)

    spans(tiles, edge)

    def place_cols(t):
        q = pl.ds(pl.multiple_of(t * TB, TB), TB)
        acc = cacc[:, q]
        for k in range(tiles):
            acc += same(blocks_ref[1, k], t) * ecol[k]
        cacc[:, q] = acc

    spans(cacc.shape[1] // TB, place_cols)

    def rows_done(slot):
        d = ORDER[slot]
        parts = []
        for h in range(2):
            acc = racc[pl.ds(slot * 256 + h * TB, TB), :]
            for k in range(tiles):
                acc += same(blocks_ref[0, k], (z + NZ - d) % NZ * 2 + h) * erow[k]
            parts.append(acc)
        return jnp.concatenate(parts, axis=0).T[0:OROWS]

    rget = {}

    def rows_out(slot):
        e = (NZ - ORDER[slot]) % NZ
        zout[e] = rows_done(slot)
        rget[e] = send(zout.at[e], zin.at[e], rz_send.at[e], rz_recv.at[e], zs[e])

    cget, xget = {}, {}

    def cols_other(d):
        src = columns(cacc, chip(d) * 2 + 1 - core, width)
        cget[d] = send(src, sib.at[d], cf_send.at[d], cf_recv.at[d], sibling)

    def cols_out(d):
        cget[d].wait_recv()
        xbuf[d] = columns(cacc, chip(d) * 2 + core, width)[...] + sib[d]
        xget[d] = send(xbuf.at[d], xin.at[d], cx_send.at[d], cx_recv.at[d], xs[d])

    def cols_of(d, first, n):
        spans(n, lambda i: unit(first + i, chip(d) * 2 + 1 - core))
        cols_other(d)
        spans(n, lambda i: unit(first + i, chip(d) * 2 + core))
        cols_out(d)

    rows_out(0)
    rows_out(1)
    cols_of(2, 1, 3)
    spans(6, lambda i: unit(1, chip(3 + i // 2) * 2 + i % 2))
    rows_out(2)
    rows_out(3)
    cols_of(1, 2, 2)
    cols_of(3, 2, 2)
    spans(2, lambda i: unit(2, x * 2 + (core + 1 + i) % 2))
    rows_out(4)
    rows_out(5)
    unit(3, x * 2 + 1 - core)
    cols_other(0)
    unit(3, x * 2 + core)
    rows_out(6)

    total = rows_done(7)
    for e in (4, 5, 3, 6, 2, 1, 7):
        rget[e].wait_recv()
        total += zin[e]
    yblk[0] = total[:, 0:128]
    yblk[1] = total[:, 128:256]
    yback = {d: send(yblk.at[(y + d) % NY // 2], yin.at[d], ry_send.at[d], ry_recv.at[d], ys[d]) for d in YD}

    cget[0].wait_recv()
    for d in XD:
        xget[d].wait_recv()
    for h in range(width // 256):
        sl = pl.ds(h * 256, 256)
        acc = columns(cacc, x * 2 + core, width)[:, sl] + sib[0, :, sl]
        for d in XD:
            acc += xin[d, :, sl]
        tot = acc[64:65]
        ng_ref[:, sl] = (acc[0:64] - npos_ref[:, sl].astype(F32) * tot) * (2.0 / n_slab)
        nb_ref[:, sl] = tot * (1.0 / n_slab)

    for d in YD:
        yback[d].wait_recv()
    own_sums = yblk[y // 2]
    for d in YD:
        own_sums += yin[d]
    odd = jnp.broadcast_to(y % 2, own_sums.shape) == 1
    own_sums = jnp.where(odd, pltpu.roll(own_sums, 64, 1), own_sums)[:, 0:64]
    tot = own_sums[64:65]
    sg_ref[...] = (spos_ref[...].astype(F32) * tot - own_sums[0:64]) * (-2.0 / n_nodes)
    sb_ref[...] = tot * (1.0 / n_nodes)
    for c in copies:
        c.wait_send()


def local(slab_pos, slab_bias, node_pos, node_bias, alpha, edge_counts, edge_blocks):
    vmem = pl.BlockSpec(memory_space=pltpu.VMEM)
    smem = pl.BlockSpec(memory_space=pltpu.SMEM)
    hbm = pl.BlockSpec(memory_space=pl.ANY)
    dma = pltpu.SemaphoreType.DMA
    own_rows, own_cols = slab_pos.shape[1], node_pos.shape[1]
    rows = own_rows * lax.axis_size("col")
    cols = own_cols * lax.axis_size("row")
    n_slab = rows * lax.axis_size("row")
    n_nodes = cols * lax.axis_size("col")
    tiles = edge_counts.shape[0]
    piece = pltpu.VMEM((NX, OROWS, own_cols), F32)
    group = pltpu.VMEM((NZ, OROWS, 256), F32)
    sg, sb, ng, nb = pl.pallas_call(
        functools.partial(body, n_nodes=n_nodes, n_slab=n_slab),
        out_shape=(
            jax.ShapeDtypeStruct((64, own_rows), F32), jax.ShapeDtypeStruct((1, own_rows), F32),
            jax.ShapeDtypeStruct((64, own_cols), F32), jax.ShapeDtypeStruct((1, own_cols), F32),
        ),
        in_specs=[smem, smem, vmem, vmem, hbm, hbm, hbm],
        out_specs=(vmem,) * 4,
        scratch_shapes=[
            pltpu.VMEM(slab_pos.shape, BF16), pltpu.VMEM(node_pos.shape, BF16),
            pltpu.VMEM(edge_counts.shape, jnp.int32), dma((3,)),
            pltpu.VMEM((KROWS, rows), BF16), pltpu.VMEM((KROWS, cols), BF16), pltpu.VMEM((cols // TB, TB, 128), BF16),
            pltpu.VMEM((rows // TB, KROWS, TB), BF16),
            pltpu.VMEM((rows, 256), BF16), pltpu.VMEM((rows, 128), F32), pltpu.VMEM((OROWS, cols), F32),
            pltpu.VMEM((tiles, TB, 128), F32), pltpu.VMEM((tiles, OROWS, TB), F32),
            pltpu.VMEM((NY, KROWS, 128), BF16), piece, piece, piece, group, group,
            pltpu.VMEM((2, OROWS, 128), F32), pltpu.VMEM((NY, OROWS, 128), F32),
        ] + [dma((NX,))] * 4 + [dma((NY,))] * 2 + [dma((NZ,))] * 2
        + [dma((NX,))] * 4 + [dma((NZ,))] * 2 + [dma((NY,))] * 2,
        compiler_params=params(collective_id=0, has_side_effects=True),
        name="gradient",
    )(
        edge_blocks.T, alpha.reshape(1, 1), slab_bias.reshape(1, own_rows), node_bias.reshape(own_cols // 128, 128),
        slab_pos, node_pos, edge_counts,
    )
    return sg, sb.reshape(own_rows), ng, nb.reshape(own_cols)


def solution(mesh):
    in_specs = (
        P(None, ("row", "col")),
        P(("row", "col")),
        P(None, ("col", "row")),
        P(("col", "row")),
        P(),
        P(("row", "col"), None, None),
        P(("row", "col"), None),
    )
    out_specs = (
        P(None, ("row", "col")),
        P(("row", "col")),
        P(None, ("col", "row")),
        P(("col", "row")),
    )
    return jax.shard_map(local, mesh=mesh, in_specs=in_specs, out_specs=out_specs, check_vma=False)
```

```python
import functools

import jax
import jax.numpy as jnp
from jax import lax
from jax.experimental import pallas as pl
from jax.experimental.pallas import tpu as pltpu
from jax.sharding import PartitionSpec as P

MESH = pl.DeviceIdType.MESH
F32 = jnp.float32
BF16 = jnp.bfloat16
LOG2E = 1.4426950408889634
NX, NY, NZ = 4, 4, 8
XD = YD = (1, 3, 2)
XNEAR = (1, 3)
ZD = (1, 7, 2, 6, 3, 5, 4)
ORDER = (4, 3, 5, 2, 6, 7, 1, 0)
SLOT = {d: s for s, d in enumerate(ORDER)}
PB, QB = 512, 1024
TB = 128
KROWS = 80
VMEM_LIMIT = 56 * 1024 * 1024


def split3(v):
    a = v.astype(BF16).astype(F32)
    b = (v - a).astype(BF16).astype(F32)
    c = (v - a - b).astype(BF16).astype(F32)
    return a, b, c


def extras(scalars):
    a, b, c = split3(scalars)
    i = lax.broadcasted_iota(jnp.int32, (16, scalars.shape[1]), 0)
    one = jnp.where((i == 0) | (i == 4) | (i == 5), 1.0, 0.0)
    ext = jnp.where(i == 1, a, jnp.where(i == 2, b, jnp.where(i == 3, c, one)))
    return ext.astype(BF16)


def position():
    row, col = lax.axis_index("row"), lax.axis_index("col")
    return row // 2, row % 2, col % NY, col // NY


def enter(peers):
    barrier = pltpu.get_barrier_semaphore()
    for peer in peers:
        pl.semaphore_signal(barrier, inc=1, device_id=peer, device_id_type=MESH)
    pl.semaphore_wait(barrier, len(peers))


def all_peers():
    x, core, y, z = position()
    row, col = lax.axis_index("row"), lax.axis_index("col")
    xs = {d: {"row": (x + d) % NX * 2 + core, "col": col} for d in XD}
    sibling = {"row": x * 2 + 1 - core, "col": col}
    ys = {d: {"row": row, "col": z * NY + (y + d) % NY} for d in YD}
    zs = {d: {"row": row, "col": (z + d) % NZ * NY + y} for d in ZD}
    return xs, sibling, ys, zs


def remote(src, dst, ssem, rsem, peer):
    return pltpu.make_async_remote_copy(
        src_ref=src, dst_ref=dst, send_sem=ssem, recv_sem=rsem, device_id=peer, device_id_type=MESH
    )


def columns(ref, index, width):
    return ref.at[:, pl.ds(pl.multiple_of(index * width, 128), width)]


def params(**kw):
    return pltpu.CompilerParams(vmem_limit_bytes=VMEM_LIMIT, **kw)


def less(a, b):
    return jnp.minimum(jnp.maximum(b - a, 0), 1)


def same(a, b):
    return 1 - jnp.minimum((a - b) * (a - b), 1)


def body(
    blocks_hbm, alpha_hbm, sbias_hbm, nbias_hbm, spos_hbm, npos_hbm, counts_hbm,
    sg_ref, sb_ref, ng_ref, nb_ref,
    blocks_ref, alpha_ref, sbias_ref, nbias_ref, spos_ref, npos_ref, counts_ref, in_sem,
    order_ref, start_ref,
    s_ref, n_ref, nt_ref, st_ref, a_ref, racc, cacc, erow, ecol,
    ypiece, sib, xbuf, xin, zout, zin, yblk, yin,
    n_send, n_recv, f_send, f_recv, y_send, y_recv, z_send, z_recv,
    cf_send, cf_recv, cx_send, cx_recv, rz_send, rz_recv, ry_send, ry_recv,
    *, n_nodes, n_slab,
):
    x, core, y, z = position()
    xs, sibling, ys, zs = all_peers()
    width = npos_ref.shape[1]
    tiles = counts_ref.shape[0]
    copies = []

    def send(src, dst, ssem, rsem, peer):
        c = remote(src, dst, ssem, rsem, peer)
        c.start()
        copies.append(c)
        return c

    loads = [
        pltpu.make_async_copy(a, b, in_sem.at[i])
        for i, (a, b) in enumerate((
            (spos_hbm, spos_ref), (sbias_hbm, sbias_ref), (alpha_hbm, alpha_ref), (npos_hbm, npos_ref),
            (nbias_hbm, nbias_ref), (blocks_hbm, blocks_ref), (counts_hbm, counts_ref),
        ))
    ]
    for c in loads:
        c.start()
    enter([xs[d] for d in XD] + [sibling] + [ys[d] for d in YD] + [zs[d] for d in ZD])

    for c in loads[0:3]:
        c.wait()
    sp = spos_ref[...].astype(F32)
    u = LOG2E * (alpha_ref[0, 0] + sbias_ref[...].astype(F32) - jnp.sum(sp * sp, axis=0, keepdims=True))
    ypiece[y] = jnp.zeros((KROWS, 128), BF16)
    ypiece[y, 0:64, 0:64] = spos_ref[...]
    ypiece[y, 64:80, 0:64] = extras(u)
    yget = {d: send(ypiece.at[y], ypiece.at[y], y_send.at[d], y_recv.at[d], ys[d]) for d in YD}

    for c in loads[3:5]:
        c.wait()
    nodes = npos_ref[...].astype(F32)
    nb = nbias_ref[...].astype(F32)
    nb = jnp.concatenate([nb[i : i + 1] for i in range(width // 128)], axis=1)
    v = LOG2E * (nb - jnp.sum(nodes * nodes, axis=0, keepdims=True))
    mine = columns(n_ref, x * 2 + core, width)
    mine[0:64, :] = npos_ref[...]
    mine[64:80, :] = extras(v)
    for d in XNEAR:
        send(mine, mine, n_send.at[d], n_recv.at[d], xs[d])
    f0 = send(mine, mine, f_send.at[0], f_recv.at[0], sibling)

    def spans(n, f):
        def step(i, _):
            f(i)
            return 0

        lax.fori_loop(0, n, step, 0)

    for c in loads[5:7]:
        c.wait()

    def key(i, k):
        return blocks_ref[i, k] * tiles + k

    def ranks(k):
        for i in range(2):
            mykey = key(i, k)
            r = less(key(i, 0), mykey)
            for j in range(1, tiles):
                r += less(key(i, j), mykey)
            order_ref[2 + i, k] = r

    def orders(m):
        for i in range(2):
            r = 0
            for k in range(tiles):
                r += k * same(order_ref[2 + i, k], m)
            order_ref[i, m] = r

    def starts(t):
        for i in range(2):
            r = less(blocks_ref[i, 0], t)
            for k in range(1, tiles):
                r += less(blocks_ref[i, k], t)
            start_ref[i, t] = r

    racc[...] = jnp.zeros_like(racc)
    cacc[...] = jnp.zeros_like(cacc)
    spans(tiles, ranks)
    spans(tiles, orders)
    spans(start_ref.shape[1], starts)

    for d in YD:
        yget[d].wait_recv()
    lane = lax.broadcasted_iota(jnp.int32, (KROWS, 128), 1)
    own = s_ref.at[:, pl.ds(SLOT[0] * 256, 256)]
    for h in range(2):
        a, b = ypiece[2 * h].astype(F32), ypiece[2 * h + 1].astype(F32)
        own[:, h * 128 : h * 128 + 128] = jnp.where(lane < 64, a, pltpu.roll(b, 64, 1)).astype(BF16)
    zget = {}
    for d in ORDER[:-1]:
        dst = s_ref.at[:, pl.ds(SLOT[d] * 256, 256)]
        zget[d] = send(own, dst, z_send.at[d], z_recv.at[d], zs[d])

    def chip(d):
        return (x + d) % NX

    near, far = 1 + 2 * core, 3 - 2 * core

    def npiece(d, k):
        return columns(n_ref, chip(NX - d) * 2 + k, width)

    def npass(d):
        remote(npiece(d, core), npiece(d, core), n_send.at[d], n_recv.at[d], sibling).wait_recv()
        remote(npiece(d, core), npiece(d, core), f_send.at[d], f_recv.at[d], sibling).start()

    remote(npiece(near, core), npiece(near, core), n_send.at[near], n_recv.at[near], sibling).wait_recv()
    onward = {"row": chip(near) * 2 + core, "col": lax.axis_index("col")}
    send(npiece(near, core), npiece(near, core), n_send.at[2], n_recv.at[2], onward)
    remote(npiece(near, core), npiece(near, core), f_send.at[near], f_recv.at[near], sibling).start()
    npass(far)

    def prep_rows(slot):
        sl = pl.ds(slot * 256, 256)
        s = s_ref[:, sl].astype(F32)
        h1, h2, h3 = split3(s[0:64] * (2.0 * LOG2E))
        k = lax.broadcasted_iota(jnp.int32, (16, 256), 0)
        one = jnp.where((k >= 1) & (k <= 3), 1.0, 0.0)
        e = jnp.where(k == 0, s[65:66], jnp.where(k == 4, s[66:67], jnp.where(k == 5, s[67:68], one)))
        t = jnp.concatenate([h1, h2, h3, e, jnp.zeros((48, 256), F32)], axis=0)
        a_ref[sl, :] = t.T.astype(BF16)

    def prep_cols(j):
        n = columns(n_ref, j, width)[...]
        t = jnp.concatenate([n.astype(F32), jnp.zeros((48, width), F32)], axis=0).T.astype(BF16)
        nt_ref[pl.ds(j * (width // TB), width // TB)] = t.reshape(width // TB, TB, 128)

    def sweep(row, n_rows, column, n_cols):
        q = pl.ds(pl.multiple_of(column, 128), n_cols)
        sl = pl.ds(pl.multiple_of(row, 128), n_rows)
        n = n_ref[:, q]
        b = jnp.concatenate([n[0:64], n[0:64], n, jnp.zeros((48, n_cols), BF16)], axis=0)
        t = jnp.dot(a_ref[sl, :], b, preferred_element_type=F32)
        lam = jnp.exp2(t).astype(BF16)
        nt = nt_ref[pl.ds(column // TB, n_cols // TB)].reshape(n_cols, 128)
        racc[sl, :] -= jnp.dot(lam, nt, preferred_element_type=F32)
        cacc[:, q] -= jnp.dot(s_ref[:, sl], lam, preferred_element_type=F32)

    def pair(p, j):
        sweep(p * 512, 512, j * width, width)

    def single(slot, c):
        sweep(slot * 256, 256, c * (2 * width), 2 * width)

    prep_rows(SLOT[0])
    f0.wait_recv()
    prep_cols(x * 2)
    prep_cols(x * 2 + 1)

    def nready(d):
        remote(npiece(d, core), npiece(d, core), f_send.at[d], f_recv.at[d], sibling).wait_recv()

    def own_first(i):
        d = 1 + 2 * i - 3 * (i // 2)

        @pl.when(i == 0)
        def _():
            nready(1)
            nready(3)

        @pl.when(i == 2)
        def _():
            npass(2)
            nready(2)

        c = chip(NX - d)
        prep_cols(c * 2)
        prep_cols(c * 2 + 1)
        single(SLOT[0], c)

    spans(3, own_first)
    for d in XD:
        copies.append(remote(npiece(d, core), npiece(d, core), f_send.at[d], f_recv.at[d], sibling))

    for d in ORDER[0:2]:
        zget[d].wait_recv()
        prep_rows(SLOT[d])
    spans(8, lambda i: pair(0, (x * 2 + i) % 8))
    for d in ORDER[2:-1]:
        zget[d].wait_recv()
        prep_rows(SLOT[d])

    for d in ORDER:
        for h in range(2):
            st_ref[(z + NZ - d) % NZ * 2 + h] = s_ref[:, pl.ds(SLOT[d] * 256 + h * TB, TB)]
    erow[0] = jnp.zeros((TB, 128), F32)
    ecol[0] = jnp.zeros((KROWS, TB), F32)

    def edge(g):
        rsum, csum = erow[g * 4], ecol[g * 4]
        for i in range(4):
            m = g * 4 + i
            k = order_ref[0, m]
            yk = counts_ref[k].astype(F32).astype(BF16)
            rsum += jnp.dot(yk, nt_ref[blocks_ref[1, k]], preferred_element_type=F32)
            erow[m + 1] = rsum
            k = order_ref[1, m]
            yk = counts_ref[k].astype(F32).astype(BF16)
            csum += jnp.dot(st_ref[blocks_ref[0, k]], yk, preferred_element_type=F32)
            ecol[m + 1] = csum

    spans(tiles // 4, edge)

    def place_cols(g):
        for i in range(4):
            t = g * 4 + i
            cacc[:, pl.ds(pl.multiple_of(t * TB, TB), TB)] += ecol[start_ref[1, t + 1]] - ecol[start_ref[1, t]]

    spans(cacc.shape[1] // TB // 4, place_cols)

    def centred(sums, pos):
        return jnp.concatenate([sums[0:64] - pos[0:64].astype(F32) * sums[64:65], sums[64:80]], axis=0)

    def rows_done(slot):
        parts = []
        for h in range(2):
            t = (z + NZ - ORDER[slot]) % NZ * 2 + h
            acc = racc[pl.ds(slot * 256 + h * TB, TB), :]
            parts.append(acc + erow[start_ref[0, t + 1]] - erow[start_ref[0, t]])
        return centred(jnp.concatenate(parts, axis=0).T[0:KROWS], s_ref[:, pl.ds(slot * 256, 256)])

    rget = {}

    def rows_out(slot):
        e = (NZ - ORDER[slot]) % NZ
        zout[e] = rows_done(slot).astype(BF16)
        rget[e] = send(zout.at[e], zin.at[e], rz_send.at[e], rz_recv.at[e], zs[e])

    cget, xget = {}, {}

    def cols_other(d):
        src = columns(cacc, chip(d) * 2 + 1 - core, width)
        cget[d] = send(src, sib.at[d], cf_send.at[d], cf_recv.at[d], sibling)

    def cols_out(d):
        j = chip(d) * 2 + core
        cget[d].wait_recv()
        for h in range(width // 256):
            sl = pl.ds(h * 256, 256)
            sums = columns(cacc, j, width)[:, sl] + sib[d, :, sl]
            xbuf[d, :, sl] = centred(sums, columns(n_ref, j, width)[:, sl]).astype(BF16)
        xget[d] = send(xbuf.at[d], xin.at[d], cx_send.at[d], cx_recv.at[d], xs[d])

    def cols_of(d, first, n):
        single(6, chip(d))
        spans(n, lambda i: pair(first + i, chip(d) * 2 + 1 - core))
        cols_other(d)
        spans(n, lambda i: pair(first + i, chip(d) * 2 + core))
        cols_out(d)

    rows_out(0)
    rows_out(1)
    cols_of(2, 1, 2)
    spans(6, lambda i: pair(1, chip(3 + i // 2) * 2 + i % 2))
    rows_out(2)
    rows_out(3)
    cols_of(1, 2, 1)
    cols_of(3, 2, 1)
    spans(2, lambda i: pair(2, x * 2 + i))
    rows_out(4)
    rows_out(5)
    single(6, x)
    rows_out(6)
    single(7, x)
    cols_other(0)

    total = rows_done(7)
    for e in (4, 5, 3, 6, 2, 1, 7):
        rget[e].wait_recv()
        total += zin[e].astype(F32)
    yblk[0] = total[:, 0:128]
    yblk[1] = total[:, 128:256]
    yback = {d: send(yblk.at[(y + d) % NY // 2], yin.at[d], ry_send.at[d], ry_recv.at[d], ys[d]) for d in YD}

    cget[0].wait_recv()
    for d in XD:
        xget[d].wait_recv()
    for h in range(width // 256):
        sl = pl.ds(h * 256, 256)
        acc = centred(columns(cacc, x * 2 + core, width)[:, sl] + sib[0, :, sl], npos_ref[:, sl])
        for d in XD:
            acc += xin[d, :, sl].astype(F32)
        ng_ref[:, sl] = acc[0:64] * (2.0 / n_slab)
        nb_ref[:, sl] = acc[64:65] * (1.0 / n_slab)

    for d in YD:
        yback[d].wait_recv()
    own_sums = yblk[y // 2]
    for d in YD:
        own_sums += yin[d]
    odd = jnp.broadcast_to(y % 2, own_sums.shape) == 1
    own_sums = jnp.where(odd, pltpu.roll(own_sums, 64, 1), own_sums)[:, 0:64]
    sg_ref[...] = own_sums[0:64] * (2.0 / n_nodes)
    sb_ref[...] = own_sums[64:65] * (1.0 / n_nodes)
    for c in copies:
        c.wait_send()


def local(slab_pos, slab_bias, node_pos, node_bias, alpha, edge_counts, edge_blocks):
    vmem = pl.BlockSpec(memory_space=pltpu.VMEM)
    hbm = pl.BlockSpec(memory_space=pltpu.HBM)
    dma = pltpu.SemaphoreType.DMA
    own_rows, own_cols = slab_pos.shape[1], node_pos.shape[1]
    rows = own_rows * lax.axis_size("col")
    cols = own_cols * lax.axis_size("row")
    n_slab = rows * lax.axis_size("row")
    n_nodes = cols * lax.axis_size("col")
    tiles = edge_counts.shape[0]
    pieces = [pltpu.VMEM((NX, KROWS, own_cols), t) for t in (F32, BF16, BF16)]
    group = pltpu.VMEM((NZ, KROWS, 256), BF16)
    sg, sb, ng, nb = pl.pallas_call(
        functools.partial(body, n_nodes=n_nodes, n_slab=n_slab),
        out_shape=(
            jax.ShapeDtypeStruct((64, own_rows), F32), jax.ShapeDtypeStruct((1, own_rows), F32),
            jax.ShapeDtypeStruct((64, own_cols), F32), jax.ShapeDtypeStruct((1, own_cols), F32),
        ),
        in_specs=[hbm] * 7,
        out_specs=(vmem,) * 4,
        scratch_shapes=[
            pltpu.SMEM((2, tiles), jnp.int32), pltpu.SMEM((1, 1), F32), pltpu.VMEM((1, own_rows), BF16),
            pltpu.VMEM((own_cols // 128, 128), BF16), pltpu.VMEM(slab_pos.shape, BF16), pltpu.VMEM(node_pos.shape, BF16),
            pltpu.VMEM(edge_counts.shape, jnp.int32), dma((7,)),
            pltpu.SMEM((4, tiles), jnp.int32), pltpu.SMEM((2, cols // TB + 1), jnp.int32),
            pltpu.VMEM((KROWS, rows), BF16), pltpu.VMEM((KROWS, cols), BF16), pltpu.VMEM((cols // TB, TB, 128), BF16),
            pltpu.VMEM((rows // TB, KROWS, TB), BF16),
            pltpu.VMEM((rows, 256), BF16), pltpu.VMEM((rows, 128), F32), pltpu.VMEM((KROWS, cols), F32),
            pltpu.VMEM((tiles + 1, TB, 128), F32), pltpu.VMEM((tiles + 1, KROWS, TB), F32),
            pltpu.VMEM((NY, KROWS, 128), BF16), *pieces, group, group,
            pltpu.VMEM((2, KROWS, 128), F32), pltpu.VMEM((NY, KROWS, 128), F32),
        ] + [dma((NX,))] * 4 + [dma((NY,))] * 2 + [dma((NZ,))] * 2
        + [dma((NX,))] * 4 + [dma((NZ,))] * 2 + [dma((NY,))] * 2,
        compiler_params=params(collective_id=0, has_side_effects=True),
        name="gradient",
    )(
        edge_blocks.T, alpha.reshape(1, 1), slab_bias.reshape(1, own_rows), node_bias.reshape(own_cols // 128, 128),
        slab_pos, node_pos, edge_counts,
    )
    return sg, sb.reshape(own_rows), ng, nb.reshape(own_cols)


def solution(mesh):
    in_specs = (
        P(None, ("row", "col")),
        P(("row", "col")),
        P(None, ("col", "row")),
        P(("col", "row")),
        P(),
        P(("row", "col"), None, None),
        P(("row", "col"), None),
    )
    out_specs = (
        P(None, ("row", "col")),
        P(("row", "col")),
        P(None, ("col", "row")),
        P(("col", "row")),
    )
    return jax.shard_map(local, mesh=mesh, in_specs=in_specs, out_specs=out_specs, check_vma=False)
```

```python
import functools

import jax
import jax.numpy as jnp
from jax import lax
from jax.experimental import pallas as pl
from jax.experimental.pallas import tpu as pltpu
from jax.sharding import PartitionSpec as P

MESH = pl.DeviceIdType.MESH
F32 = jnp.float32
BF16 = jnp.bfloat16
LOG2E = 1.4426950408889634
NX, NY, NZ = 4, 4, 8
XD = YD = (1, 3, 2)
XNEAR = (1, 3)
ZD = (1, 7, 2, 6, 3, 5, 4)
ORDER = (2, 6, 3, 5, 1, 7, 4, 0)
ZSEND = (2, 6, 3, 5, 4, 1, 7)
LATE = (1, 7)
PIECE = 40
SLOT = {d: s for s, d in enumerate(ORDER)}

TB = 128
KROWS = 80
OROWS = 72
VMEM_LIMIT = 56 * 1024 * 1024


def split3(v):
    a = v.astype(BF16).astype(F32)
    b = (v - a).astype(BF16).astype(F32)
    c = (v - a - b).astype(BF16).astype(F32)
    return a, b, c


def extras(scalars):
    a, b, c = split3(scalars)
    i = lax.broadcasted_iota(jnp.int32, (16, scalars.shape[1]), 0)
    one = jnp.where((i == 0) | (i == 4) | (i == 5), 1.0, 0.0)
    ext = jnp.where(i == 1, a, jnp.where(i == 2, b, jnp.where(i == 3, c, one)))
    return ext.astype(BF16)


def position():
    row, col = lax.axis_index("row"), lax.axis_index("col")
    return row // 2, row % 2, col % NY, col // NY


def enter(peers):
    barrier = pltpu.get_barrier_semaphore()
    for peer in peers:
        pl.semaphore_signal(barrier, inc=1, device_id=peer, device_id_type=MESH)
    pl.semaphore_wait(barrier, len(peers))


def all_peers():
    x, core, y, z = position()
    row, col = lax.axis_index("row"), lax.axis_index("col")
    xs = {d: {"row": (x + d) % NX * 2 + core, "col": col} for d in XD}
    sibling = {"row": x * 2 + 1 - core, "col": col}
    ys = {d: {"row": row, "col": z * NY + (y + d) % NY} for d in YD}
    zs = {d: {"row": row, "col": (z + d) % NZ * NY + y} for d in ZD}
    return xs, sibling, ys, zs


def remote(src, dst, ssem, rsem, peer):
    return pltpu.make_async_remote_copy(
        src_ref=src, dst_ref=dst, send_sem=ssem, recv_sem=rsem, device_id=peer, device_id_type=MESH
    )


def columns(ref, index, width):
    return ref.at[:, pl.ds(pl.multiple_of(index * width, 128), width)]


def params(**kw):
    return pltpu.CompilerParams(vmem_limit_bytes=VMEM_LIMIT, **kw)


def below(a, b):
    return lax.shift_right_arithmetic(a - b, 31)


def body(
    blocks_hbm, alpha_hbm, sbias_hbm, nbias_hbm, spos_hbm, npos_hbm, counts_hbm,
    rout_ref, cout_ref,
    blocks_ref, alpha_ref, sbias_ref, nbias_ref, spos_ref, npos_ref, counts_ref, in_sem,
    order_ref, start_ref,
    s_ref, n_ref, nt_ref, st_ref, a_ref, racc, cacc, erow, ecol,
    ypiece, sib, xbuf, xin, zout, zin, lout, lin, yblk, yin,
    n_send, n_recv, f_send, f_recv, y_send, y_recv, z_send, z_recv,
    cf_send, cf_recv, cx_send, cx_recv, rz_send, rz_recv, l_send, l_recv, ry_send, ry_recv,
):
    x, core, y, z = position()
    xs, sibling, ys, zs = all_peers()
    width = npos_ref.shape[1]
    tiles = counts_ref.shape[0]
    copies = []

    def send(src, dst, ssem, rsem, peer):
        c = remote(src, dst, ssem, rsem, peer)
        c.start()
        copies.append(c)
        return c

    loads = [
        pltpu.make_async_copy(a, b, in_sem.at[i])
        for i, (a, b) in enumerate((
            (spos_hbm, spos_ref), (sbias_hbm, sbias_ref), (alpha_hbm, alpha_ref), (npos_hbm, npos_ref),
            (nbias_hbm, nbias_ref), (blocks_hbm, blocks_ref), (counts_hbm, counts_ref),
        ))
    ]
    for c in loads:
        c.start()
    corners = [
        {"row": lax.axis_index("row"), "col": (z + e) % NZ * NY + (y + d) % NY} for e in LATE for d in YD
    ]
    enter([xs[d] for d in XD] + [sibling] + [ys[d] for d in YD] + [zs[d] for d in ZD] + corners)

    for c in loads[0:3]:
        c.wait()
    sp = spos_ref[...].astype(F32)
    u = LOG2E * (alpha_ref[0, 0] + sbias_ref[...].astype(F32) - jnp.sum(sp * sp, axis=0, keepdims=True))
    ypiece[y] = jnp.zeros((KROWS, 128), BF16)
    ypiece[y, 0:64, 0:64] = spos_ref[...]
    ypiece[y, 64:80, 0:64] = extras(u)
    yget = {d: send(ypiece.at[y], ypiece.at[y], y_send.at[d], y_recv.at[d], ys[d]) for d in YD}

    for c in loads[3:5]:
        c.wait()
    nodes = npos_ref[...].astype(F32)
    nb = nbias_ref[...].astype(F32)
    nb = jnp.concatenate([nb[i : i + 1] for i in range(width // 128)], axis=1)
    v = LOG2E * (nb - jnp.sum(nodes * nodes, axis=0, keepdims=True))
    mine = columns(n_ref, x * 2 + core, width)
    mine[0:64, :] = npos_ref[...]
    mine[64:80, :] = extras(v)
    for d in XNEAR:
        send(mine, mine, n_send.at[d], n_recv.at[d], xs[d])
    f0 = send(mine, mine, f_send.at[0], f_recv.at[0], sibling)

    def spans(n, f):
        def step(i, _):
            f(i)
            return 0

        lax.fori_loop(0, n, step, 0)

    for c in loads[5:7]:
        c.wait()

    def sort(i, n_blocks):
        block = [blocks_ref[i, k] for k in range(tiles)]
        keys = [b * tiles + k for k, b in enumerate(block)]
        rank = [jnp.int32(k) for k in range(tiles)]
        for k in range(tiles):
            for j in range(k):
                r = 1 + below(keys[j], keys[k])
                rank[k] = rank[k] - r
                rank[j] = rank[j] + r

        for k in range(tiles):
            order_ref[2 + i, k] = rank[k]

        def orders(m):
            r = 0
            for k in range(1, tiles):
                d = order_ref[2 + i, k] - m
                r += k - k * jnp.minimum(d * d, 1)
            order_ref[i, m] = r

        spans(tiles, orders)

        def starts(t):
            r = 0
            for b in block:
                r -= below(b, t)
            start_ref[i, t] = r

        spans(n_blocks + 1, starts)

    racc[...] = jnp.zeros_like(racc)
    cacc[...] = jnp.zeros_like(cacc)
    sort(0, racc.shape[0] // TB)
    sort(1, cacc.shape[1] // TB)

    for d in YD:
        yget[d].wait_recv()
    lane = lax.broadcasted_iota(jnp.int32, (KROWS, 128), 1)
    own = s_ref.at[:, pl.ds(SLOT[0] * 256, 256)]
    for h in range(2):
        a, b = ypiece[2 * h].astype(F32), ypiece[2 * h + 1].astype(F32)
        own[:, h * 128 : h * 128 + 128] = jnp.where(lane < 64, a, pltpu.roll(b, 64, 1)).astype(BF16)
    zget = {}
    for d in ZSEND:
        dst = s_ref.at[:, pl.ds(SLOT[d] * 256, 256)]
        zget[d] = send(own, dst, z_send.at[d], z_recv.at[d], zs[d])

    def chip(d):
        return (x + d) % NX

    near, far = 1 + 2 * core, 3 - 2 * core

    def npiece(d, k):
        return columns(n_ref, chip(NX - d) * 2 + k, width)

    def npass(d):
        remote(npiece(d, core), npiece(d, core), n_send.at[d], n_recv.at[d], sibling).wait_recv()
        remote(npiece(d, core), npiece(d, core), f_send.at[d], f_recv.at[d], sibling).start()

    def prep_rows(slot):
        sl = pl.ds(slot * 256, 256)
        s = s_ref[:, sl].astype(F32)
        h1, h2, h3 = split3(s[0:64] * (2.0 * LOG2E))
        k = lax.broadcasted_iota(jnp.int32, (16, 256), 0)
        one = jnp.where((k >= 1) & (k <= 3), 1.0, 0.0)
        e = jnp.where(k == 0, s[65:66], jnp.where(k == 4, s[66:67], jnp.where(k == 5, s[67:68], one)))
        t = jnp.concatenate([h1, h2, h3, e, jnp.zeros((48, 256), F32)], axis=0)
        a_ref[sl, :] = t.T.astype(BF16)

    def prep_cols(j):
        n = columns(n_ref, j, width)[...]
        t = jnp.concatenate([n.astype(F32), jnp.zeros((48, width), F32)], axis=0).T.astype(BF16)
        nt_ref[pl.ds(j * (width // TB), width // TB)] = t.reshape(width // TB, TB, 128)

    def sweep(row, n_rows, column, n_cols):
        q = pl.ds(pl.multiple_of(column, 128), n_cols)
        sl = pl.ds(pl.multiple_of(row, 128), n_rows)
        n = n_ref[:, q]
        b = jnp.concatenate([n[0:64], n[0:64], n, jnp.zeros((48, n_cols), BF16)], axis=0)
        t = jnp.dot(a_ref[sl, :], b, preferred_element_type=F32)
        lam = jnp.exp2(t).astype(BF16)
        nt = nt_ref[pl.ds(column // TB, n_cols // TB)].reshape(n_cols, 128)
        racc[sl, :] -= jnp.dot(lam, nt, preferred_element_type=F32)
        cacc[:, q] -= jnp.dot(s_ref[:, sl], lam, preferred_element_type=F32)

    def pair(p, j):
        sweep(p * 512, 512, j * width, width)

    def single(slot, c):
        sweep(slot * 256, 256, c * (2 * width), 2 * width)

    prep_rows(SLOT[0])
    f0.wait_recv()
    prep_cols(x * 2)
    prep_cols(x * 2 + 1)
    single(SLOT[0], x)
    remote(npiece(near, core), npiece(near, core), n_send.at[near], n_recv.at[near], sibling).wait_recv()
    onward = {"row": chip(near) * 2 + core, "col": lax.axis_index("col")}
    send(npiece(near, core), npiece(near, core), n_send.at[2], n_recv.at[2], onward)
    remote(npiece(near, core), npiece(near, core), f_send.at[near], f_recv.at[near], sibling).start()
    npass(far)


    def nready(d):
        remote(npiece(d, core), npiece(d, core), f_send.at[d], f_recv.at[d], sibling).wait_recv()

    def own_near(i):
        d = 1 + 2 * i
        nready(d)
        c = chip(NX - d)
        prep_cols(c * 2)
        prep_cols(c * 2 + 1)
        single(SLOT[0], c)

    spans(2, own_near)
    for d in ORDER[0:2]:
        zget[d].wait_recv()
        prep_rows(SLOT[d])
    spans(2, lambda i: pair(0, x * 2 + i))
    npass(2)
    spans(4, lambda i: pair(0, chip(3 + i // 2 * 2) * 2 + i % 2))
    nready(2)
    for d in XD:
        copies.append(remote(npiece(d, core), npiece(d, core), f_send.at[d], f_recv.at[d], sibling))
    prep_cols(chip(2) * 2)
    prep_cols(chip(2) * 2 + 1)
    single(SLOT[0], chip(2))
    spans(2, lambda i: pair(0, chip(2) * 2 + i))
    for d in ORDER[2:-1]:
        zget[d].wait_recv()
        prep_rows(SLOT[d])

    for d in ORDER:
        for h in range(2):
            st_ref[(z + NZ - d) % NZ * 2 + h] = s_ref[:, pl.ds(SLOT[d] * 256 + h * TB, TB)]
    erow[0] = jnp.zeros((TB, 128), F32)
    ecol[0] = jnp.zeros((KROWS, TB), F32)

    def edge(g):
        rsum, csum = erow[g * 4], ecol[g * 4]
        for i in range(4):
            m = g * 4 + i
            k = order_ref[0, m]
            yk = counts_ref[k].astype(F32).astype(BF16)
            rsum += jnp.dot(yk, nt_ref[blocks_ref[1, k]], preferred_element_type=F32)
            erow[m + 1] = rsum
            k = order_ref[1, m]
            yk = counts_ref[k].astype(F32).astype(BF16)
            csum += jnp.dot(st_ref[blocks_ref[0, k]], yk, preferred_element_type=F32)
            ecol[m + 1] = csum

    spans(tiles // 4, edge)

    def place_cols(g):
        for i in range(4):
            t = g * 4 + i
            cacc[:, pl.ds(pl.multiple_of(t * TB, TB), TB)] += ecol[start_ref[1, t + 1]] - ecol[start_ref[1, t]]

    spans(cacc.shape[1] // TB // 4, place_cols)

    def centred(sums, pos):
        return jnp.concatenate([sums[0:64] - pos[0:64].astype(F32) * sums[64:65], sums[64:80]], axis=0)

    def rows_done(slot):
        parts = []
        for h in range(2):
            t = (z + NZ - ORDER[slot]) % NZ * 2 + h
            acc = racc[pl.ds(slot * 256 + h * TB, TB), :]
            parts.append(acc + erow[start_ref[0, t + 1]] - erow[start_ref[0, t]])
        return centred(jnp.concatenate(parts, axis=0).T[0:KROWS], s_ref[:, pl.ds(slot * 256, 256)])

    rget = {}

    def rows_out(slot):
        e = (NZ - ORDER[slot]) % NZ
        zout[e] = rows_done(slot).astype(BF16)
        rget[e] = send(zout.at[e], zin.at[e], rz_send.at[e], rz_recv.at[e], zs[e])

    def pack(block):
        lane = lax.broadcasted_iota(jnp.int32, (PIECE, 128), 1)
        out = []
        for h in range(2):
            top, low = block[0:PIECE, h * 128 : h * 128 + 128], block[PIECE:KROWS, h * 128 : h * 128 + 128]
            out.append(jnp.where(lane < 64, top, pltpu.roll(low, 64, 1)))
            out.append(jnp.where(lane < 64, pltpu.roll(top, 64, 1), low))
        return out

    late = {}

    def rows_late(i):
        e = NZ - LATE[i]
        for t, p in enumerate(pack(rows_done(SLOT[LATE[i]]))):
            lout[i, t] = p
        for d in range(NY):
            peer = {"row": lax.axis_index("row"), "col": (z + e) % NZ * NY + (y + d) % NY}
            late[i, d] = send(lout.at[i, (y + d) % NY], lin.at[i, d], l_send.at[i, d], l_recv.at[i, d], peer)

    cget, xget = {}, {}

    def cols_other(d):
        src = columns(cacc, chip(d) * 2 + 1 - core, width).at[0:OROWS]
        cget[d] = send(src, sib.at[d], cf_send.at[d], cf_recv.at[d], sibling)

    def cols_sum(d):
        cget[d].wait_recv()
        xbuf[d] = columns(cacc, chip(d) * 2 + core, width)[0:OROWS] + sib[d]

    def cols_out(d):
        cols_sum(d)

        @pl.when(near == d)
        def _():
            relayed.wait_recv()
            xbuf[d] += xin[2]

        xget[d] = send(xbuf.at[d], xin.at[d], cx_send.at[d], cx_recv.at[d], xs[d])

    def cols_units(d, first, n, k):
        spans(n, lambda i: pair(first + i, chip(d) * 2 + k))

    rows_out(0)
    rows_out(1)
    single(6, chip(2))
    cols_units(2, 1, 2, 1 - core)
    cols_other(2)
    cols_units(2, 1, 2, core)
    cols_sum(2)
    relayed = send(xbuf.at[2], xin.at[2], cx_send.at[2], cx_recv.at[2], onward)
    spans(3, lambda i: single(6, chip(3 + i)))
    rows_out(6)
    spans(6, lambda i: pair(1, chip(3 + i // 2) * 2 + i % 2))
    rows_out(2)
    rows_out(3)
    for d in XNEAR:
        cols_units(d, 2, 1, 1 - core)
        cols_other(d)
        cols_units(d, 2, 1, core)
        cols_out(d)
    cols_units(0, 2, 1, 1 - core)
    cols_other(0)
    cols_units(0, 2, 1, core)
    rows_late(0)
    rows_late(1)

    total = rows_done(7)
    for e in (6, 2, 4, 5, 3):
        rget[e].wait_recv()
        total += zin[e].astype(F32)
    for t, p in enumerate(pack(total)):
        yblk[t] = p
    yback = {d: send(yblk.at[(y + d) % NY], yin.at[d], ry_send.at[d], ry_recv.at[d], ys[d]) for d in YD}

    cget[0].wait_recv()
    for d in XNEAR:
        xget[d].wait_recv()
    for h in range(width // 256):
        sl = pl.ds(h * 256, 256)
        acc = columns(cacc, x * 2 + core, width)[0:OROWS, sl] + sib[0, :, sl]
        acc += xin[1, :, sl] + xin[3, :, sl]
        cout_ref[:, sl] = acc

    own_sums = yblk[y]
    for key in late:
        late[key].wait_recv()
        own_sums += lin[key]
    for d in YD:
        yback[d].wait_recv()
        own_sums += yin[d]
    rout_ref[...] = own_sums
    for c in copies:
        c.wait_send()


def finish(npos_ref, rows_ref, cols_ref, sg_ref, sb_ref, ng_ref, nb_ref, *, n_nodes, n_slab):
    r = rows_ref[...]
    low = pltpu.roll(r, 64, 1)
    sums = jnp.concatenate([r, low], axis=0)[:, 0:64]
    sg_ref[...] = sums[0:64] * (2.0 / n_nodes)
    sb_ref[...] = sums[64:65] * (1.0 / n_nodes)
    tot = cols_ref[64:65, :]
    ng_ref[...] = (cols_ref[0:64, :] - npos_ref[...].astype(F32) * tot) * (2.0 / n_slab)
    nb_ref[...] = tot * (1.0 / n_slab)


def local(slab_pos, slab_bias, node_pos, node_bias, alpha, edge_counts, edge_blocks):
    vmem = pl.BlockSpec(memory_space=pltpu.VMEM)
    hbm = pl.BlockSpec(memory_space=pltpu.HBM)
    dma = pltpu.SemaphoreType.DMA
    own_rows, own_cols = slab_pos.shape[1], node_pos.shape[1]
    rows = own_rows * lax.axis_size("col")
    cols = own_cols * lax.axis_size("row")
    n_slab = rows * lax.axis_size("row")
    n_nodes = cols * lax.axis_size("col")
    tiles = edge_counts.shape[0]
    pieces = [pltpu.VMEM((NX, OROWS, own_cols), F32)] * 3
    group = pltpu.VMEM((NZ, KROWS, 256), BF16)
    row_sums, col_sums = pl.pallas_call(
        body,
        out_shape=(jax.ShapeDtypeStruct((PIECE, 128), F32), jax.ShapeDtypeStruct((OROWS, own_cols), F32)),
        in_specs=[hbm] * 7,
        out_specs=(vmem,) * 2,
        scratch_shapes=[
            pltpu.SMEM((2, tiles), jnp.int32), pltpu.SMEM((1, 1), F32), pltpu.VMEM((1, own_rows), BF16),
            pltpu.VMEM((own_cols // 128, 128), BF16), pltpu.VMEM(slab_pos.shape, BF16), pltpu.VMEM(node_pos.shape, BF16),
            pltpu.VMEM(edge_counts.shape, jnp.int32), dma((7,)),
            pltpu.SMEM((4, tiles), jnp.int32), pltpu.SMEM((2, cols // TB + 1), jnp.int32),
            pltpu.VMEM((KROWS, rows), BF16), pltpu.VMEM((KROWS, cols), BF16), pltpu.VMEM((cols // TB, TB, 128), BF16),
            pltpu.VMEM((rows // TB, KROWS, TB), BF16),
            pltpu.VMEM((rows, 256), BF16), pltpu.VMEM((rows, 128), F32), pltpu.VMEM((KROWS, cols), F32),
            pltpu.VMEM((tiles + 1, TB, 128), F32), pltpu.VMEM((tiles + 1, KROWS, TB), F32),
            pltpu.VMEM((NY, KROWS, 128), BF16), *pieces, group, group,
            pltpu.VMEM((2, NY, PIECE, 128), F32), pltpu.VMEM((2, NY, PIECE, 128), F32),
            pltpu.VMEM((NY, PIECE, 128), F32), pltpu.VMEM((NY, PIECE, 128), F32),
        ] + [dma((NX,))] * 4 + [dma((NY,))] * 2 + [dma((NZ,))] * 2
        + [dma((NX,))] * 4 + [dma((NZ,))] * 2 + [dma((2, NY))] * 2 + [dma((NY,))] * 2,
        compiler_params=params(collective_id=0, has_side_effects=True),
        name="gradient",
    )(
        edge_blocks.T, alpha.reshape(1, 1), slab_bias.reshape(1, own_rows), node_bias.reshape(own_cols // 128, 128),
        slab_pos, node_pos, edge_counts,
    )
    sg, sb, ng, nb = pl.pallas_call(
        functools.partial(finish, n_nodes=n_nodes, n_slab=n_slab),
        out_shape=(
            jax.ShapeDtypeStruct((64, own_rows), F32), jax.ShapeDtypeStruct((1, own_rows), F32),
            jax.ShapeDtypeStruct((64, own_cols), F32), jax.ShapeDtypeStruct((1, own_cols), F32),
        ),
        in_specs=[vmem] * 3,
        out_specs=(vmem,) * 4,
        compiler_params=params(),
        name="finish",
    )(node_pos, row_sums, col_sums)
    return sg, sb.reshape(own_rows), ng, nb.reshape(own_cols)


def solution(mesh):
    in_specs = (
        P(None, ("row", "col")),
        P(("row", "col")),
        P(None, ("col", "row")),
        P(("col", "row")),
        P(),
        P(("row", "col"), None, None),
        P(("row", "col"), None),
    )
    out_specs = (
        P(None, ("row", "col")),
        P(("row", "col")),
        P(None, ("col", "row")),
        P(("col", "row")),
    )
    return jax.shard_map(local, mesh=mesh, in_specs=in_specs, out_specs=out_specs, check_vma=False)
```

```python
import functools

import jax
import jax.numpy as jnp
from jax import lax
from jax.experimental import pallas as pl
from jax.experimental.pallas import tpu as pltpu
from jax.sharding import PartitionSpec as P

MESH = pl.DeviceIdType.MESH
F32 = jnp.float32
BF16 = jnp.bfloat16
LOG2E = 1.4426950408889634
NX, NY, NZ = 4, 4, 8
XD = YD = (1, 3, 2)
XNEAR = (1, 3)
ZD = (1, 7, 2, 6, 3, 5, 4)
ORDER = (2, 6, 3, 5, 1, 7, 4, 0)
ZSEND = (2, 6, 3, 5, 4, 1, 7)
LATE = (1, 7)
PIECE = 40
SLOT = {d: s for s, d in enumerate(ORDER)}

TB = 128
KROWS = 80
OROWS = 72
VMEM_LIMIT = 56 * 1024 * 1024


def split3(v):
    a = v.astype(BF16).astype(F32)
    b = (v - a).astype(BF16).astype(F32)
    c = (v - a - b).astype(BF16).astype(F32)
    return a, b, c


def extras(scalars):
    a, b, c = split3(scalars)
    i = lax.broadcasted_iota(jnp.int32, (16, scalars.shape[1]), 0)
    one = jnp.where((i == 0) | (i == 4) | (i == 5), 1.0, 0.0)
    ext = jnp.where(i == 1, a, jnp.where(i == 2, b, jnp.where(i == 3, c, one)))
    return ext.astype(BF16)


def position():
    row, col = lax.axis_index("row"), lax.axis_index("col")
    return row // 2, row % 2, col % NY, col // NY


def greet(peers):
    for peer in peers:
        pl.semaphore_signal(pltpu.get_barrier_semaphore(), inc=1, device_id=peer, device_id_type=MESH)


def all_peers():
    x, core, y, z = position()
    row, col = lax.axis_index("row"), lax.axis_index("col")
    xs = {d: {"row": (x + d) % NX * 2 + core, "col": col} for d in XD}
    sibling = {"row": x * 2 + 1 - core, "col": col}
    ys = {d: {"row": row, "col": z * NY + (y + d) % NY} for d in YD}
    zs = {d: {"row": row, "col": (z + d) % NZ * NY + y} for d in ZD}
    return xs, sibling, ys, zs


def remote(src, dst, ssem, rsem, peer):
    return pltpu.make_async_remote_copy(
        src_ref=src, dst_ref=dst, send_sem=ssem, recv_sem=rsem, device_id=peer, device_id_type=MESH
    )


def columns(ref, index, width):
    return ref.at[:, pl.ds(pl.multiple_of(index * width, 128), width)]


def params(**kw):
    return pltpu.CompilerParams(vmem_limit_bytes=VMEM_LIMIT, **kw)


def tile_tables(keys, tiles):
    lane = lax.broadcasted_iota(jnp.int32, (tiles, 128), 1)
    tile = lax.broadcasted_iota(jnp.int32, (tiles, 128), 0)
    column = keys.T
    orders, starts = [], []
    for i in range(2):
        k = jnp.broadcast_to(column[0:tiles, i : i + 1], (tiles, 128))
        j = jnp.broadcast_to(keys[i : i + 1, :], (tiles, 128))
        before = jnp.where((lane < tiles) & ((j < k) | ((j == k) & (lane < tile))), 1, 0)
        rank = jnp.broadcast_to(jnp.sum(before, axis=1, keepdims=True), (tiles, 128))
        here = jnp.where(rank == lane, tile, 0)
        orders.append(jnp.sum(here, axis=0, keepdims=True))
        starts.append(jnp.sum(jnp.where(k < lane, 1, 0), axis=0, keepdims=True))
    return jnp.concatenate(orders + starts + [jnp.zeros((4, 128), jnp.int32)], axis=0)


def body(
    blocks_hbm, alpha_hbm, sbias_hbm, nbias_hbm, spos_hbm, npos_hbm, counts_hbm,
    rout_ref, cout_ref,
    blocks_ref, alpha_ref, sbias_ref, nbias_ref, spos_ref, npos_ref, counts_ref, in_sem,
    bvec_ref, table_ref, order_ref,
    s_ref, n_ref, nt_ref, st_ref, a_ref, racc, cacc, erow, ecol,
    ypiece, sib, xbuf, xin, zout, zin, lout, lin, yblk, yin,
    n_send, n_recv, f_send, f_recv, y_send, y_recv, z_send, z_recv,
    cf_send, cf_recv, cx_send, cx_recv, rz_send, rz_recv, l_send, l_recv, ry_send, ry_recv,
):
    x, core, y, z = position()
    xs, sibling, ys, zs = all_peers()
    width = npos_ref.shape[1]
    tiles = counts_ref.shape[0]
    copies = []

    def send(src, dst, ssem, rsem, peer):
        c = remote(src, dst, ssem, rsem, peer)
        c.start()
        copies.append(c)
        return c

    loads = [
        pltpu.make_async_copy(a, b, in_sem.at[i])
        for i, (a, b) in enumerate((
            (spos_hbm, spos_ref), (sbias_hbm, sbias_ref), (alpha_hbm, alpha_ref), (npos_hbm, npos_ref),
            (nbias_hbm, nbias_ref), (blocks_hbm, blocks_ref),
            (blocks_hbm, bvec_ref), (counts_hbm, counts_ref),
        ))
    ]
    for c in loads:
        c.start()
    corners = [
        {"row": lax.axis_index("row"), "col": (z + e) % NZ * NY + (y + d) % NY} for e in LATE for d in YD
    ]
    peers = [xs[d] for d in XD] + [sibling] + [ys[d] for d in YD] + [zs[d] for d in ZD] + corners
    greet(peers)

    for c in loads[0:3]:
        c.wait()
    sp = spos_ref[...].astype(F32)
    u = LOG2E * (alpha_ref[0, 0] + sbias_ref[...].astype(F32) - jnp.sum(sp * sp, axis=0, keepdims=True))
    ypiece[y] = jnp.zeros((KROWS, 128), BF16)
    ypiece[y, 0:64, 0:64] = spos_ref[...]
    ypiece[y, 64:80, 0:64] = extras(u)

    for c in loads[3:5]:
        c.wait()
    nodes = npos_ref[...].astype(F32)
    nb = nbias_ref[...].astype(F32)
    nb = jnp.concatenate([nb[i : i + 1] for i in range(width // 128)], axis=1)
    v = LOG2E * (nb - jnp.sum(nodes * nodes, axis=0, keepdims=True))
    mine = columns(n_ref, x * 2 + core, width)
    mine[0:64, :] = npos_ref[...]
    mine[64:80, :] = extras(v)
    pl.semaphore_wait(pltpu.get_barrier_semaphore(), len(peers))
    yget = {d: send(ypiece.at[y], ypiece.at[y], y_send.at[d], y_recv.at[d], ys[d]) for d in YD}
    for d in XNEAR:
        send(mine, mine, n_send.at[d], n_recv.at[d], xs[d])
    f0 = send(mine, mine, f_send.at[0], f_recv.at[0], sibling)

    def spans(n, f):
        def step(i, _):
            f(i)
            return 0

        lax.fori_loop(0, n, step, 0)

    for c in loads[5:8]:
        c.wait()

    racc[...] = jnp.zeros_like(racc)
    cacc[...] = jnp.zeros_like(cacc)
    table_ref[...] = jnp.zeros_like(table_ref)
    table_ref[0:2, 0:tiles] = bvec_ref[...]
    table_ref[...] = tile_tables(table_ref[...], tiles)
    tables = pltpu.make_async_copy(table_ref, order_ref, in_sem.at[8])
    tables.start()

    for d in YD:
        yget[d].wait_recv()
    lane = lax.broadcasted_iota(jnp.int32, (KROWS, 128), 1)
    own = s_ref.at[:, pl.ds(SLOT[0] * 256, 256)]
    for h in range(2):
        a, b = ypiece[2 * h].astype(F32), ypiece[2 * h + 1].astype(F32)
        own[:, h * 128 : h * 128 + 128] = jnp.where(lane < 64, a, pltpu.roll(b, 64, 1)).astype(BF16)
    zget = {}
    for d in ZSEND:
        dst = s_ref.at[:, pl.ds(SLOT[d] * 256, 256)]
        zget[d] = send(own, dst, z_send.at[d], z_recv.at[d], zs[d])

    def chip(d):
        return (x + d) % NX

    near, far = 1 + 2 * core, 3 - 2 * core

    def npiece(d, k):
        return columns(n_ref, chip(NX - d) * 2 + k, width)

    def npass(d):
        remote(npiece(d, core), npiece(d, core), n_send.at[d], n_recv.at[d], sibling).wait_recv()
        remote(npiece(d, core), npiece(d, core), f_send.at[d], f_recv.at[d], sibling).start()

    def prep_rows(slot):
        sl = pl.ds(slot * 256, 256)
        s = s_ref[:, sl].astype(F32)
        h1, h2, h3 = split3(s[0:64] * (2.0 * LOG2E))
        k = lax.broadcasted_iota(jnp.int32, (16, 256), 0)
        one = jnp.where((k >= 1) & (k <= 3), 1.0, 0.0)
        e = jnp.where(k == 0, s[65:66], jnp.where(k == 4, s[66:67], jnp.where(k == 5, s[67:68], one)))
        t = jnp.concatenate([h1, h2, h3, e, jnp.zeros((48, 256), F32)], axis=0)
        a_ref[sl, :] = t.astype(BF16).T

    def prep_cols(j):
        n = columns(n_ref, j, width)[...]
        t = jnp.concatenate([n, jnp.zeros((48, width), BF16)], axis=0).T
        nt_ref[pl.ds(j * (width // TB), width // TB)] = t.reshape(width // TB, TB, 128)

    def sweep(row, n_rows, column, n_cols):
        q = pl.ds(pl.multiple_of(column, 128), n_cols)
        sl = pl.ds(pl.multiple_of(row, 128), n_rows)
        n = n_ref[:, q]
        b = jnp.concatenate([n[0:64], n[0:64], n, jnp.zeros((48, n_cols), BF16)], axis=0)
        t = jnp.dot(a_ref[sl, :], b, preferred_element_type=F32)
        lam = jnp.exp2(t).astype(BF16)
        nt = nt_ref[pl.ds(column // TB, n_cols // TB)].reshape(n_cols, 128)
        racc[sl, :] -= jnp.dot(lam, nt, preferred_element_type=F32)
        cacc[:, q] -= jnp.dot(s_ref[:, sl], lam, preferred_element_type=F32)

    def pair(p, j):
        sweep(p * 512, 512, j * width, width)

    def single(slot, c):
        sweep(slot * 256, 256, c * (2 * width), 2 * width)

    prep_rows(SLOT[0])
    f0.wait_recv()
    prep_cols(x * 2)
    prep_cols(x * 2 + 1)
    single(SLOT[0], x)
    remote(npiece(near, core), npiece(near, core), n_send.at[near], n_recv.at[near], sibling).wait_recv()
    onward = {"row": chip(near) * 2 + core, "col": lax.axis_index("col")}
    send(npiece(near, core), npiece(near, core), n_send.at[2], n_recv.at[2], onward)
    remote(npiece(near, core), npiece(near, core), f_send.at[near], f_recv.at[near], sibling).start()
    npass(far)


    def nready(d):
        remote(npiece(d, core), npiece(d, core), f_send.at[d], f_recv.at[d], sibling).wait_recv()

    def own_near(i):
        d = 1 + 2 * i
        nready(d)
        c = chip(NX - d)
        prep_cols(c * 2)
        prep_cols(c * 2 + 1)
        single(SLOT[0], c)

    spans(2, own_near)
    for d in ORDER[0:2]:
        zget[d].wait_recv()
        prep_rows(SLOT[d])
    spans(2, lambda i: pair(0, x * 2 + i))
    npass(2)
    spans(4, lambda i: pair(0, chip(3 + i // 2 * 2) * 2 + i % 2))
    nready(2)
    for d in XD:
        copies.append(remote(npiece(d, core), npiece(d, core), f_send.at[d], f_recv.at[d], sibling))
    prep_cols(chip(2) * 2)
    prep_cols(chip(2) * 2 + 1)
    single(SLOT[0], chip(2))
    spans(2, lambda i: pair(0, chip(2) * 2 + i))
    for d in ORDER[2:-1]:
        zget[d].wait_recv()
        prep_rows(SLOT[d])

    for d in ORDER:
        for h in range(2):
            st_ref[(z + NZ - d) % NZ * 2 + h] = s_ref[:, pl.ds(SLOT[d] * 256 + h * TB, TB)]
    tables.wait()
    erow[0] = jnp.zeros((TB, 128), F32)
    ecol[0] = jnp.zeros((KROWS, TB), F32)

    def entry(row, at, most):
        return jnp.minimum(jnp.maximum(order_ref[row, at], 0), most)

    def edge(g):
        rsum, csum = erow[g * 4], ecol[g * 4]
        for i in range(4):
            m = g * 4 + i
            k = entry(0, m, tiles - 1)
            yk = counts_ref[k].astype(F32).astype(BF16)
            rsum += jnp.dot(yk, nt_ref[blocks_ref[1, k]], preferred_element_type=F32)
            erow[m + 1] = rsum
            k = entry(1, m, tiles - 1)
            yk = counts_ref[k].astype(F32).astype(BF16)
            csum += jnp.dot(st_ref[blocks_ref[0, k]], yk, preferred_element_type=F32)
            ecol[m + 1] = csum

    spans(tiles // 4, edge)

    def place_cols(g):
        for i in range(4):
            t = g * 4 + i
            cacc[:, pl.ds(pl.multiple_of(t * TB, TB), TB)] += ecol[entry(3, t + 1, tiles)] - ecol[entry(3, t, tiles)]

    spans(cacc.shape[1] // TB // 4, place_cols)

    def centred(sums, pos):
        return jnp.concatenate([sums[0:64] - pos[0:64].astype(F32) * sums[64:65], sums[64:80]], axis=0)

    def rows_done(slot):
        parts = []
        for h in range(2):
            t = (z + NZ - ORDER[slot]) % NZ * 2 + h
            acc = racc[pl.ds(slot * 256 + h * TB, TB), :]
            parts.append(acc + erow[entry(2, t + 1, tiles)] - erow[entry(2, t, tiles)])
        return centred(jnp.concatenate(parts, axis=0).T[0:KROWS], s_ref[:, pl.ds(slot * 256, 256)])

    rget = {}

    def rows_out(slot):
        e = (NZ - ORDER[slot]) % NZ
        zout[e] = rows_done(slot).astype(BF16)
        rget[e] = send(zout.at[e], zin.at[e], rz_send.at[e], rz_recv.at[e], zs[e])

    def pack(block):
        lane = lax.broadcasted_iota(jnp.int32, (PIECE, 128), 1)
        out = []
        for h in range(2):
            top, low = block[0:PIECE, h * 128 : h * 128 + 128], block[PIECE:KROWS, h * 128 : h * 128 + 128]
            out.append(jnp.where(lane < 64, top, pltpu.roll(low, 64, 1)))
            out.append(jnp.where(lane < 64, pltpu.roll(top, 64, 1), low))
        return out

    late = {}

    def rows_late(i):
        e = NZ - LATE[i]
        for t, p in enumerate(pack(rows_done(SLOT[LATE[i]]))):
            lout[i, t, 0:PIECE] = p.astype(BF16)
        for d in range(NY):
            peer = {"row": lax.axis_index("row"), "col": (z + e) % NZ * NY + (y + d) % NY}
            late[i, d] = send(lout.at[i, (y + d) % NY], lin.at[i, d], l_send.at[i, d], l_recv.at[i, d], peer)

    cget, xget = {}, {}

    def cols_other(d):
        src = columns(cacc, chip(d) * 2 + 1 - core, width).at[0:OROWS]
        cget[d] = send(src, sib.at[d], cf_send.at[d], cf_recv.at[d], sibling)

    def cols_sum(d):
        cget[d].wait_recv()
        xbuf[d] = columns(cacc, chip(d) * 2 + core, width)[0:OROWS] + sib[d]

    def cols_out(d):
        cols_sum(d)

        @pl.when(near == d)
        def _():
            relayed.wait_recv()
            xbuf[d] += xin[2]

        xget[d] = send(xbuf.at[d], xin.at[d], cx_send.at[d], cx_recv.at[d], xs[d])

    def cols_units(d, first, n, k):
        spans(n, lambda i: pair(first + i, chip(d) * 2 + k))

    rows_out(0)
    rows_out(1)
    single(6, chip(2))
    cols_units(2, 1, 2, 1 - core)
    cols_other(2)
    cols_units(2, 1, 2, core)
    spans(3, lambda i: single(6, chip(3 + i)))
    rows_out(6)
    cols_sum(2)
    relayed = send(xbuf.at[2], xin.at[2], cx_send.at[2], cx_recv.at[2], onward)
    spans(6, lambda i: pair(1, chip(3 + i // 2) * 2 + i % 2))
    rows_out(2)
    rows_out(3)
    for d in XNEAR:
        cols_units(d, 2, 1, 1 - core)
        cols_other(d)
    for d in XNEAR:
        cols_units(d, 2, 1, core)
        cols_out(d)
    single(4, x)
    rows_late(0)

    total = rows_done(7)
    for e in (6, 2, 4, 5, 3):
        rget[e].wait_recv()
        total += zin[e].astype(F32)
    for t, p in enumerate(pack(total)):
        yblk[t] = p
    yback = {d: send(yblk.at[(y + d) % NY], yin.at[d], ry_send.at[d], ry_recv.at[d], ys[d]) for d in YD}
    single(5, x)
    cols_other(0)
    rows_late(1)

    for d in XNEAR:
        xget[d].wait_recv()
    cget[0].wait_recv()
    for h in range(width // 256):
        sl = pl.ds(h * 256, 256)
        acc = columns(cacc, x * 2 + core, width)[0:OROWS, sl] + sib[0, :, sl]
        acc += xin[1, :, sl] + xin[3, :, sl]
        cout_ref[:, sl] = acc

    own_sums = yblk[y]
    for key in late:
        late[key].wait_recv()
        own_sums += lin[key][0:PIECE].astype(F32)
    for d in YD:
        yback[d].wait_recv()
        own_sums += yin[d]
    rout_ref[...] = own_sums
    for c in copies:
        c.wait_send()


def finish(npos_ref, rows_ref, cols_ref, sg_ref, sb_ref, ng_ref, nb_ref, *, n_nodes, n_slab):
    r = rows_ref[...]
    low = pltpu.roll(r, 64, 1)
    sums = jnp.concatenate([r, low], axis=0)[:, 0:64]
    sg_ref[...] = sums[0:64] * (2.0 / n_nodes)
    sb_ref[...] = sums[64:65] * (1.0 / n_nodes)
    tot = cols_ref[64:65, :]
    ng_ref[...] = (cols_ref[0:64, :] - npos_ref[...].astype(F32) * tot) * (2.0 / n_slab)
    nb_ref[...] = tot * (1.0 / n_slab)


def local(slab_pos, slab_bias, node_pos, node_bias, alpha, edge_counts, edge_blocks):
    vmem = pl.BlockSpec(memory_space=pltpu.VMEM)
    hbm = pl.BlockSpec(memory_space=pltpu.HBM)
    dma = pltpu.SemaphoreType.DMA
    own_rows, own_cols = slab_pos.shape[1], node_pos.shape[1]
    rows = own_rows * lax.axis_size("col")
    cols = own_cols * lax.axis_size("row")
    n_slab = rows * lax.axis_size("row")
    n_nodes = cols * lax.axis_size("col")
    tiles = edge_counts.shape[0]
    pieces = [pltpu.VMEM((NX, OROWS, own_cols), F32)] * 3
    group = pltpu.VMEM((NZ, KROWS, 256), BF16)
    row_sums, col_sums = pl.pallas_call(
        body,
        out_shape=(jax.ShapeDtypeStruct((PIECE, 128), F32), jax.ShapeDtypeStruct((OROWS, own_cols), F32)),
        in_specs=[hbm] * 7,
        out_specs=(vmem,) * 2,
        scratch_shapes=[
            pltpu.SMEM((2, tiles), jnp.int32), pltpu.SMEM((1, 1), F32), pltpu.VMEM((1, own_rows), BF16),
            pltpu.VMEM((own_cols // 128, 128), BF16), pltpu.VMEM(slab_pos.shape, BF16), pltpu.VMEM(node_pos.shape, BF16),
            pltpu.VMEM(edge_counts.shape, jnp.int32), dma((9,)),
            pltpu.VMEM((2, tiles), jnp.int32), pltpu.VMEM((8, 128), jnp.int32), pltpu.SMEM((8, 128), jnp.int32),
            pltpu.VMEM((KROWS, rows), BF16), pltpu.VMEM((KROWS, cols), BF16), pltpu.VMEM((cols // TB, TB, 128), BF16),
            pltpu.VMEM((rows // TB, KROWS, TB), BF16),
            pltpu.VMEM((rows, 256), BF16), pltpu.VMEM((rows, 128), F32), pltpu.VMEM((KROWS, cols), F32),
            pltpu.VMEM((tiles + 1, TB, 128), F32), pltpu.VMEM((tiles + 1, KROWS, TB), F32),
            pltpu.VMEM((NY, KROWS, 128), BF16), *pieces, group, group,
            pltpu.VMEM((2, NY, 48, 128), BF16), pltpu.VMEM((2, NY, 48, 128), BF16),
            pltpu.VMEM((NY, PIECE, 128), F32), pltpu.VMEM((NY, PIECE, 128), F32),
        ] + [dma((NX,))] * 4 + [dma((NY,))] * 2 + [dma((NZ,))] * 2
        + [dma((NX,))] * 4 + [dma((NZ,))] * 2 + [dma((2, NY))] * 2 + [dma((NY,))] * 2,
        compiler_params=params(collective_id=0, has_side_effects=True),
        name="gradient",
    )(
        edge_blocks.T, alpha.reshape(1, 1), slab_bias.reshape(1, own_rows), node_bias.reshape(own_cols // 128, 128),
        slab_pos, node_pos, edge_counts,
    )
    sg, sb, ng, nb = pl.pallas_call(
        functools.partial(finish, n_nodes=n_nodes, n_slab=n_slab),
        out_shape=(
            jax.ShapeDtypeStruct((64, own_rows), F32), jax.ShapeDtypeStruct((1, own_rows), F32),
            jax.ShapeDtypeStruct((64, own_cols), F32), jax.ShapeDtypeStruct((1, own_cols), F32),
        ),
        in_specs=[vmem] * 3,
        out_specs=(vmem,) * 4,
        compiler_params=params(),
        name="finish",
    )(node_pos, row_sums, col_sums)
    return sg, sb.reshape(own_rows), ng, nb.reshape(own_cols)


def solution(mesh):
    in_specs = (
        P(None, ("row", "col")),
        P(("row", "col")),
        P(None, ("col", "row")),
        P(("col", "row")),
        P(),
        P(("row", "col"), None, None),
        P(("row", "col"), None),
    )
    out_specs = (
        P(None, ("row", "col")),
        P(("row", "col")),
        P(None, ("col", "row")),
        P(("col", "row")),
    )
    return jax.shard_map(local, mesh=mesh, in_specs=in_specs, out_specs=out_specs, check_vma=False)
```

```python
import functools

import jax
import jax.numpy as jnp
from jax import lax
from jax.experimental import pallas as pl
from jax.experimental.pallas import tpu as pltpu
from jax.sharding import PartitionSpec as P

MESH = pl.DeviceIdType.MESH
F32 = jnp.float32
BF16 = jnp.bfloat16
LOG2E = 1.4426950408889634
NX, NY, NZ = 4, 4, 8
XD = YD = (1, 3, 2)
XNEAR = (1, 3)
ZD = (1, 7, 2, 6, 3, 5, 4)
ORDER = (2, 6, 5, 3, 1, 7, 4, 0)
ZSEND = (2, 6, 3, 5, 4, 1, 7)
LATE = (5, 3, 1, 7)
PIECE = 40
SLOT = {d: s for s, d in enumerate(ORDER)}

TB = 128
KROWS = 80
OROWS = 72
VMEM_LIMIT = 56 * 1024 * 1024


def split3(v):
    a = v.astype(BF16).astype(F32)
    b = (v - a).astype(BF16).astype(F32)
    c = (v - a - b).astype(BF16).astype(F32)
    return a, b, c


def extras(scalars):
    a, b, c = split3(scalars)
    i = lax.broadcasted_iota(jnp.int32, (16, scalars.shape[1]), 0)
    one = jnp.where((i == 0) | (i == 4) | (i == 5), 1.0, 0.0)
    ext = jnp.where(i == 1, a, jnp.where(i == 2, b, jnp.where(i == 3, c, one)))
    return ext.astype(BF16)


def position():
    row, col = lax.axis_index("row"), lax.axis_index("col")
    return row // 2, row % 2, col % NY, col // NY


def greet(peers):
    for peer in peers:
        pl.semaphore_signal(pltpu.get_barrier_semaphore(), inc=1, device_id=peer, device_id_type=MESH)


def all_peers():
    x, core, y, z = position()
    row, col = lax.axis_index("row"), lax.axis_index("col")
    xs = {d: {"row": (x + d) % NX * 2 + core, "col": col} for d in XD}
    sibling = {"row": x * 2 + 1 - core, "col": col}
    ys = {d: {"row": row, "col": z * NY + (y + d) % NY} for d in YD}
    zs = {d: {"row": row, "col": (z + d) % NZ * NY + y} for d in ZD}
    return xs, sibling, ys, zs


def remote(src, dst, ssem, rsem, peer):
    return pltpu.make_async_remote_copy(
        src_ref=src, dst_ref=dst, send_sem=ssem, recv_sem=rsem, device_id=peer, device_id_type=MESH
    )


def columns(ref, index, width):
    return ref.at[:, pl.ds(pl.multiple_of(index * width, 128), width)]


def params(**kw):
    return pltpu.CompilerParams(vmem_limit_bytes=VMEM_LIMIT, **kw)


def tile_tables(keys, tiles):
    lane = lax.broadcasted_iota(jnp.int32, (tiles, 128), 1)
    tile = lax.broadcasted_iota(jnp.int32, (tiles, 128), 0)
    column = keys.T
    orders, starts = [], []
    for i in range(2):
        k = jnp.broadcast_to(column[0:tiles, i : i + 1], (tiles, 128))
        j = jnp.broadcast_to(keys[i : i + 1, :], (tiles, 128))
        before = jnp.where((lane < tiles) & ((j < k) | ((j == k) & (lane < tile))), 1, 0)
        rank = jnp.broadcast_to(jnp.sum(before, axis=1, keepdims=True), (tiles, 128))
        here = jnp.where(rank == lane, tile, 0)
        orders.append(jnp.sum(here, axis=0, keepdims=True))
        starts.append(jnp.sum(jnp.where(k < lane, 1, 0), axis=0, keepdims=True))
    return jnp.concatenate(orders + starts + [jnp.zeros((4, 128), jnp.int32)], axis=0)


def body(
    blocks_hbm, alpha_hbm, sbias_hbm, nbias_hbm, spos_hbm, npos_hbm, counts_hbm,
    rout_ref, cout_ref,
    blocks_ref, alpha_ref, sbias_ref, nbias_ref, spos_ref, npos_ref, counts_ref, in_sem,
    bvec_ref, table_ref, order_ref,
    s_ref, n_ref, nt_ref, st_ref, a_ref, racc, cacc, erow, ecol,
    ypiece, sib, xbuf, xin, zout, zin, lout, lin, yblk, yin,
    n_send, n_recv, f_send, f_recv, y_send, y_recv, z_send, z_recv,
    cf_send, cf_recv, cx_send, cx_recv, rz_send, rz_recv, l_send, l_recv, ry_send, ry_recv,
):
    x, core, y, z = position()
    xs, sibling, ys, zs = all_peers()
    width = npos_ref.shape[1]
    tiles = counts_ref.shape[0]
    copies = []

    def send(src, dst, ssem, rsem, peer):
        c = remote(src, dst, ssem, rsem, peer)
        c.start()
        copies.append(c)
        return c

    loads = [
        pltpu.make_async_copy(a, b, in_sem.at[i])
        for i, (a, b) in enumerate((
            (spos_hbm, spos_ref), (sbias_hbm, sbias_ref), (alpha_hbm, alpha_ref), (npos_hbm, npos_ref),
            (nbias_hbm, nbias_ref), (blocks_hbm, blocks_ref),
            (blocks_hbm, bvec_ref), (counts_hbm, counts_ref),
        ))
    ]
    for c in loads:
        c.start()
    corners = [
        {"row": lax.axis_index("row"), "col": (z + e) % NZ * NY + (y + d) % NY} for e in LATE for d in YD
    ]
    peers = [xs[d] for d in XD] + [sibling] + [ys[d] for d in YD] + [zs[d] for d in ZD] + corners
    greet(peers)

    for c in loads[0:3]:
        c.wait()
    sp = spos_ref[...].astype(F32)
    u = LOG2E * (alpha_ref[0, 0] + sbias_ref[...].astype(F32) - jnp.sum(sp * sp, axis=0, keepdims=True))
    ypiece[y] = jnp.zeros((KROWS, 128), BF16)
    ypiece[y, 0:64, 0:64] = spos_ref[...]
    ypiece[y, 64:80, 0:64] = extras(u)

    for c in loads[3:5]:
        c.wait()
    nodes = npos_ref[...].astype(F32)
    nb = nbias_ref[...].astype(F32)
    nb = jnp.concatenate([nb[i : i + 1] for i in range(width // 128)], axis=1)
    v = LOG2E * (nb - jnp.sum(nodes * nodes, axis=0, keepdims=True))
    mine = columns(n_ref, x * 2 + core, width)
    mine[0:64, :] = npos_ref[...]
    mine[64:80, :] = extras(v)
    pl.semaphore_wait(pltpu.get_barrier_semaphore(), len(peers))
    yget = {d: send(ypiece.at[y], ypiece.at[y], y_send.at[d], y_recv.at[d], ys[d]) for d in YD}
    for d in XNEAR:
        send(mine, mine, n_send.at[d], n_recv.at[d], xs[d])
    f0 = send(mine, mine, f_send.at[0], f_recv.at[0], sibling)

    def spans(n, f):
        def step(i, _):
            f(i)
            return 0

        lax.fori_loop(0, n, step, 0)

    for c in loads[5:8]:
        c.wait()

    racc[...] = jnp.zeros_like(racc)
    cacc[...] = jnp.zeros_like(cacc)
    table_ref[...] = jnp.zeros_like(table_ref)
    table_ref[0:2, 0:tiles] = bvec_ref[...]
    table_ref[...] = tile_tables(table_ref[...], tiles)
    tables = pltpu.make_async_copy(table_ref, order_ref, in_sem.at[8])
    tables.start()

    for d in YD:
        yget[d].wait_recv()
    lane = lax.broadcasted_iota(jnp.int32, (KROWS, 128), 1)
    own = s_ref.at[:, pl.ds(SLOT[0] * 256, 256)]
    for h in range(2):
        a, b = ypiece[2 * h].astype(F32), ypiece[2 * h + 1].astype(F32)
        own[:, h * 128 : h * 128 + 128] = jnp.where(lane < 64, a, pltpu.roll(b, 64, 1)).astype(BF16)
    zget = {}
    for d in ZSEND:
        dst = s_ref.at[:, pl.ds(SLOT[d] * 256, 256)]
        zget[d] = send(own, dst, z_send.at[d], z_recv.at[d], zs[d])

    def chip(d):
        return (x + d) % NX

    near, far = 1 + 2 * core, 3 - 2 * core

    def npiece(d, k):
        return columns(n_ref, chip(NX - d) * 2 + k, width)

    def npass(d):
        remote(npiece(d, core), npiece(d, core), n_send.at[d], n_recv.at[d], sibling).wait_recv()
        remote(npiece(d, core), npiece(d, core), f_send.at[d], f_recv.at[d], sibling).start()

    def prep_rows(slot):
        sl = pl.ds(slot * 256, 256)
        s = s_ref[:, sl].astype(F32)
        h1, h2, h3 = split3(s[0:64] * (2.0 * LOG2E))
        k = lax.broadcasted_iota(jnp.int32, (16, 256), 0)
        one = jnp.where((k >= 1) & (k <= 3), 1.0, 0.0)
        e = jnp.where(k == 0, s[65:66], jnp.where(k == 4, s[66:67], jnp.where(k == 5, s[67:68], one)))
        t = jnp.concatenate([h1, h2, h3, e, jnp.zeros((48, 256), F32)], axis=0)
        a_ref[sl, :] = t.astype(BF16).T

    def prep_cols(j):
        n = columns(n_ref, j, width)[...]
        t = jnp.concatenate([n, jnp.zeros((48, width), BF16)], axis=0).T
        nt_ref[pl.ds(j * (width // TB), width // TB)] = t.reshape(width // TB, TB, 128)

    def sweep(row, n_rows, column, n_cols):
        q = pl.ds(pl.multiple_of(column, 128), n_cols)
        sl = pl.ds(pl.multiple_of(row, 128), n_rows)
        n = n_ref[:, q]
        b = jnp.concatenate([n[0:64], n[0:64], n, jnp.zeros((48, n_cols), BF16)], axis=0)
        t = jnp.dot(a_ref[sl, :], b, preferred_element_type=F32)
        lam = jnp.exp2(t).astype(BF16)
        nt = nt_ref[pl.ds(column // TB, n_cols // TB)].reshape(n_cols, 128)
        racc[sl, :] -= jnp.dot(lam, nt, preferred_element_type=F32)
        cacc[:, q] -= jnp.dot(s_ref[:, sl], lam, preferred_element_type=F32)

    def pair(c):
        sweep(0, 512, c * (2 * width), 2 * width)

    def single(slot, c):
        sweep(slot * 256, 256, c * (2 * width), 2 * width)

    prep_rows(SLOT[0])
    f0.wait_recv()
    prep_cols(x * 2)
    prep_cols(x * 2 + 1)
    single(SLOT[0], x)
    remote(npiece(near, core), npiece(near, core), n_send.at[near], n_recv.at[near], sibling).wait_recv()
    onward = {"row": chip(near) * 2 + core, "col": lax.axis_index("col")}
    send(npiece(near, core), npiece(near, core), n_send.at[2], n_recv.at[2], onward)
    remote(npiece(near, core), npiece(near, core), f_send.at[near], f_recv.at[near], sibling).start()
    npass(far)


    def nready(d):
        remote(npiece(d, core), npiece(d, core), f_send.at[d], f_recv.at[d], sibling).wait_recv()

    def own_near(i):
        d = 1 + 2 * i
        nready(d)
        c = chip(NX - d)
        prep_cols(c * 2)
        prep_cols(c * 2 + 1)
        single(SLOT[0], c)

    spans(2, own_near)
    for d in ORDER[0:2]:
        zget[d].wait_recv()
        prep_rows(SLOT[d])
    pair(x)
    npass(2)
    spans(2, lambda i: pair(chip(3 + i * 2)))
    nready(2)
    for d in XD:
        copies.append(remote(npiece(d, core), npiece(d, core), f_send.at[d], f_recv.at[d], sibling))
    prep_cols(chip(2) * 2)
    prep_cols(chip(2) * 2 + 1)
    single(SLOT[0], chip(2))
    pair(chip(2))
    for d in ORDER[2:-1]:
        zget[d].wait_recv()
        prep_rows(SLOT[d])

    for d in ORDER:
        for h in range(2):
            st_ref[(z + NZ - d) % NZ * 2 + h] = s_ref[:, pl.ds(SLOT[d] * 256 + h * TB, TB)]
    tables.wait()
    erow[0] = jnp.zeros((TB, 128), F32)
    ecol[0] = jnp.zeros((KROWS, TB), F32)

    def entry(row, at, most):
        return jnp.minimum(jnp.maximum(order_ref[row, at], 0), most)

    def edge(g):
        rsum, csum = erow[g * 4], ecol[g * 4]
        for i in range(4):
            m = g * 4 + i
            k = entry(0, m, tiles - 1)
            yk = counts_ref[k].astype(F32).astype(BF16)
            rsum += jnp.dot(yk, nt_ref[blocks_ref[1, k]], preferred_element_type=F32)
            erow[m + 1] = rsum
            k = entry(1, m, tiles - 1)
            yk = counts_ref[k].astype(F32).astype(BF16)
            csum += jnp.dot(st_ref[blocks_ref[0, k]], yk, preferred_element_type=F32)
            ecol[m + 1] = csum

    spans(tiles // 4, edge)

    def place_cols(g):
        for i in range(4):
            t = g * 4 + i
            cacc[:, pl.ds(pl.multiple_of(t * TB, TB), TB)] += ecol[entry(3, t + 1, tiles)] - ecol[entry(3, t, tiles)]

    spans(cacc.shape[1] // TB // 4, place_cols)

    def centred(sums, pos):
        return jnp.concatenate([sums[0:64] - pos[0:64].astype(F32) * sums[64:65], sums[64:80]], axis=0)

    def rows_done(slot, d):
        parts = []
        for h in range(2):
            t = (z + NZ - d) % NZ * 2 + h
            acc = racc[pl.ds(pl.multiple_of(slot * 256 + h * TB, TB), TB), :]
            parts.append(acc + erow[entry(2, t + 1, tiles)] - erow[entry(2, t, tiles)])
        return centred(jnp.concatenate(parts, axis=0).T[0:KROWS], columns(s_ref, slot, 256)[...])

    rget = {}

    def rows_out(slot):
        e = (NZ - ORDER[slot]) % NZ
        zout[e] = rows_done(slot, ORDER[slot]).astype(BF16)
        rget[e] = send(zout.at[e], zin.at[e], rz_send.at[e], rz_recv.at[e], zs[e])

    def pack(block):
        lane = lax.broadcasted_iota(jnp.int32, (PIECE, 128), 1)
        out = []
        for h in range(2):
            top, low = block[0:PIECE, h * 128 : h * 128 + 128], block[PIECE:KROWS, h * 128 : h * 128 + 128]
            out.append(jnp.where(lane < 64, top, pltpu.roll(low, 64, 1)))
            out.append(jnp.where(lane < 64, pltpu.roll(top, 64, 1), low))
        return out

    def late_copy(i, t):
        e = NZ - (13 - 2 * i) % NZ
        peer = {"row": lax.axis_index("row"), "col": (z + e) % NZ * NY + (y + t) % NY}
        return remote(lout.at[i, (y + t) % NY], lin.at[i, t], l_send.at[i, t], l_recv.at[i, t], peer)

    def rows_late(i):
        for t, p in enumerate(pack(rows_done(2 + i, (13 - 2 * i) % NZ))):
            lout[i, t, 0:PIECE] = p.astype(BF16)
        for t in range(NY):
            late_copy(i, t).start()

    def core_copy(d):
        src = columns(cacc, chip(d) * 2 + 1 - core, width).at[0:OROWS]
        return remote(src, sib.at[d], cf_send.at[d], cf_recv.at[d], sibling)

    def cols_sum(d):
        core_copy(d).wait_recv()
        xbuf[d] = columns(cacc, chip(d) * 2 + core, width)[0:OROWS] + sib[d]

    def chip_copy(d):
        peer = {"row": chip(d) * 2 + core, "col": lax.axis_index("col")}
        return remote(xbuf.at[d], xin.at[d], cx_send.at[d], cx_recv.at[d], peer)

    def four(d, k):
        sweep(512, 1024, (chip(d) * 2 + k) * width, width)

    rows_out(0)
    rows_out(1)
    single(6, chip(2))
    def far_units(i):
        four(2, (1 + core + i) % 2)

        @pl.when(i == 0)
        def _():
            core_copy(2).start()

    spans(2, far_units)
    spans(3, lambda i: single(6, chip(3 + i)))
    rows_out(6)
    cols_sum(2)
    relayed = send(xbuf.at[2], xin.at[2], cx_send.at[2], cx_recv.at[2], onward)

    def near_units(i):
        d = 1 + i % 2 * 2
        four(d, (1 + core + i // 2) % 2)

        @pl.when(i < 2)
        def _():
            core_copy(d).start()

        @pl.when(i >= 2)
        def _():
            cols_sum(d)

            @pl.when(near == d)
            def _():
                relayed.wait_recv()
                xbuf[d] += xin[2]

            chip_copy(d).start()

    spans(4, near_units)

    total = rows_done(7, 0)
    for e in (6, 2, 4):
        rget[e].wait_recv()
        total += zin[e].astype(F32)
    for t, p in enumerate(pack(total)):
        yblk[t] = p
    yback = {d: send(yblk.at[(y + d) % NY], yin.at[d], ry_send.at[d], ry_recv.at[d], ys[d]) for d in YD}

    def late_units(i):
        single(2 + i, x)

        @pl.when(i == 3)
        def _():
            core_copy(0).start()

        rows_late(i)

    spans(4, late_units)

    for d in XNEAR:
        chip_copy(d).wait_recv()
        copies.append(chip_copy(d))
    core_copy(0).wait_recv()
    for d in range(NX):
        copies.append(core_copy(d))
    for h in range(width // 256):
        sl = pl.ds(h * 256, 256)
        acc = columns(cacc, x * 2 + core, width)[0:OROWS, sl] + sib[0, :, sl]
        acc += xin[1, :, sl] + xin[3, :, sl]
        cout_ref[:, sl] = acc

    own_sums = yblk[y]
    for i in range(len(LATE)):
        for t in range(NY):
            late_copy(i, t).wait_recv()
            copies.append(late_copy(i, t))
            own_sums += lin[i, t, 0:PIECE].astype(F32)
    for d in YD:
        yback[d].wait_recv()
        own_sums += yin[d]
    rout_ref[...] = own_sums
    for c in copies:
        c.wait_send()


def finish(npos_ref, rows_ref, cols_ref, sg_ref, sb_ref, ng_ref, nb_ref, *, n_nodes, n_slab):
    r = rows_ref[...]
    low = pltpu.roll(r, 64, 1)
    sums = jnp.concatenate([r, low], axis=0)[:, 0:64]
    sg_ref[...] = sums[0:64] * (2.0 / n_nodes)
    sb_ref[...] = sums[64:65] * (1.0 / n_nodes)
    tot = cols_ref[64:65, :]
    ng_ref[...] = (cols_ref[0:64, :] - npos_ref[...].astype(F32) * tot) * (2.0 / n_slab)
    nb_ref[...] = tot * (1.0 / n_slab)


def local(slab_pos, slab_bias, node_pos, node_bias, alpha, edge_counts, edge_blocks):
    vmem = pl.BlockSpec(memory_space=pltpu.VMEM)
    hbm = pl.BlockSpec(memory_space=pltpu.HBM)
    dma = pltpu.SemaphoreType.DMA
    own_rows, own_cols = slab_pos.shape[1], node_pos.shape[1]
    rows = own_rows * lax.axis_size("col")
    cols = own_cols * lax.axis_size("row")
    n_slab = rows * lax.axis_size("row")
    n_nodes = cols * lax.axis_size("col")
    tiles = edge_counts.shape[0]
    pieces = [pltpu.VMEM((NX, OROWS, own_cols), F32)] * 3
    group = pltpu.VMEM((NZ, KROWS, 256), BF16)
    row_sums, col_sums = pl.pallas_call(
        body,
        out_shape=(jax.ShapeDtypeStruct((PIECE, 128), F32), jax.ShapeDtypeStruct((OROWS, own_cols), F32)),
        in_specs=[hbm] * 7,
        out_specs=(vmem,) * 2,
        scratch_shapes=[
            pltpu.SMEM((2, tiles), jnp.int32), pltpu.SMEM((1, 1), F32), pltpu.VMEM((1, own_rows), BF16),
            pltpu.VMEM((own_cols // 128, 128), BF16), pltpu.VMEM(slab_pos.shape, BF16), pltpu.VMEM(node_pos.shape, BF16),
            pltpu.VMEM(edge_counts.shape, jnp.int32), dma((9,)),
            pltpu.VMEM((2, tiles), jnp.int32), pltpu.VMEM((8, 128), jnp.int32), pltpu.SMEM((8, 128), jnp.int32),
            pltpu.VMEM((KROWS, rows), BF16), pltpu.VMEM((KROWS, cols), BF16), pltpu.VMEM((cols // TB, TB, 128), BF16),
            pltpu.VMEM((rows // TB, KROWS, TB), BF16),
            pltpu.VMEM((rows, 256), BF16), pltpu.VMEM((rows, 128), F32), pltpu.VMEM((KROWS, cols), F32),
            pltpu.VMEM((tiles + 1, TB, 128), F32), pltpu.VMEM((tiles + 1, KROWS, TB), F32),
            pltpu.VMEM((NY, KROWS, 128), BF16), *pieces, group, group,
            pltpu.VMEM((len(LATE), NY, 48, 128), BF16), pltpu.VMEM((len(LATE), NY, 48, 128), BF16),
            pltpu.VMEM((NY, PIECE, 128), F32), pltpu.VMEM((NY, PIECE, 128), F32),
        ] + [dma((NX,))] * 4 + [dma((NY,))] * 2 + [dma((NZ,))] * 2
        + [dma((NX,))] * 4 + [dma((NZ,))] * 2 + [dma((len(LATE), NY))] * 2 + [dma((NY,))] * 2,
        compiler_params=params(collective_id=0, has_side_effects=True),
        name="gradient",
    )(
        edge_blocks.T, alpha.reshape(1, 1), slab_bias.reshape(1, own_rows), node_bias.reshape(own_cols // 128, 128),
        slab_pos, node_pos, edge_counts,
    )
    sg, sb, ng, nb = pl.pallas_call(
        functools.partial(finish, n_nodes=n_nodes, n_slab=n_slab),
        out_shape=(
            jax.ShapeDtypeStruct((64, own_rows), F32), jax.ShapeDtypeStruct((1, own_rows), F32),
            jax.ShapeDtypeStruct((64, own_cols), F32), jax.ShapeDtypeStruct((1, own_cols), F32),
        ),
        in_specs=[vmem] * 3,
        out_specs=(vmem,) * 4,
        compiler_params=params(),
        name="finish",
    )(node_pos, row_sums, col_sums)
    return sg, sb.reshape(own_rows), ng, nb.reshape(own_cols)


def solution(mesh):
    in_specs = (
        P(None, ("row", "col")),
        P(("row", "col")),
        P(None, ("col", "row")),
        P(("col", "row")),
        P(),
        P(("row", "col"), None, None),
        P(("row", "col"), None),
    )
    out_specs = (
        P(None, ("row", "col")),
        P(("row", "col")),
        P(None, ("col", "row")),
        P(("col", "row")),
    )
    return jax.shard_map(local, mesh=mesh, in_specs=in_specs, out_specs=out_specs, check_vma=False)
```

```python
import functools

import jax
import jax.numpy as jnp
from jax import lax
from jax.experimental import pallas as pl
from jax.experimental.pallas import tpu as pltpu
from jax.sharding import PartitionSpec as P

MESH = pl.DeviceIdType.MESH
F32 = jnp.float32
BF16 = jnp.bfloat16
LOG2E = 1.4426950408889634
NX, NY, NZ = 4, 4, 8
XD = YD = (1, 3, 2)
XNEAR = (1, 3)
ZD = (1, 7, 2, 6, 3, 5, 4)
ORDER = (2, 6, 5, 3, 1, 7, 4, 0)
ZSEND = (2, 6, 3, 5, 4, 1, 7)
LATE = (1, 7)
PIECE = 40
SLOT = {d: s for s, d in enumerate(ORDER)}

TB = 128
KROWS = 80
OROWS = 72
VMEM_LIMIT = 56 * 1024 * 1024


def split3(v):
    a = v.astype(BF16).astype(F32)
    b = (v - a).astype(BF16).astype(F32)
    c = (v - a - b).astype(BF16).astype(F32)
    return a, b, c


def extras(scalars):
    a, b, c = split3(scalars)
    i = lax.broadcasted_iota(jnp.int32, (16, scalars.shape[1]), 0)
    one = jnp.where((i == 0) | (i == 4) | (i == 5), 1.0, 0.0)
    ext = jnp.where(i == 1, a, jnp.where(i == 2, b, jnp.where(i == 3, c, one)))
    return ext.astype(BF16)


def position():
    row, col = lax.axis_index("row"), lax.axis_index("col")
    return row // 2, row % 2, col % NY, col // NY


def greet(peers):
    for peer in peers:
        pl.semaphore_signal(pltpu.get_barrier_semaphore(), inc=1, device_id=peer, device_id_type=MESH)


def all_peers():
    x, core, y, z = position()
    row, col = lax.axis_index("row"), lax.axis_index("col")
    xs = {d: {"row": (x + d) % NX * 2 + core, "col": col} for d in XD}
    sibling = {"row": x * 2 + 1 - core, "col": col}
    ys = {d: {"row": row, "col": z * NY + (y + d) % NY} for d in YD}
    zs = {d: {"row": row, "col": (z + d) % NZ * NY + y} for d in ZD}
    return xs, sibling, ys, zs


def remote(src, dst, ssem, rsem, peer):
    return pltpu.make_async_remote_copy(
        src_ref=src, dst_ref=dst, send_sem=ssem, recv_sem=rsem, device_id=peer, device_id_type=MESH
    )


def columns(ref, index, width):
    return ref.at[:, pl.ds(pl.multiple_of(index * width, 128), width)]


def params(**kw):
    return pltpu.CompilerParams(vmem_limit_bytes=VMEM_LIMIT, **kw)


def tile_tables(keys, tiles):
    lane = lax.broadcasted_iota(jnp.int32, (tiles, 128), 1)
    tile = lax.broadcasted_iota(jnp.int32, (tiles, 128), 0)
    column = keys.T
    orders, starts = [], []
    for i in range(2):
        k = jnp.broadcast_to(column[0:tiles, i : i + 1], (tiles, 128))
        j = jnp.broadcast_to(keys[i : i + 1, :], (tiles, 128))
        before = jnp.where((lane < tiles) & ((j < k) | ((j == k) & (lane < tile))), 1, 0)
        rank = jnp.broadcast_to(jnp.sum(before, axis=1, keepdims=True), (tiles, 128))
        here = jnp.where(rank == lane, tile, 0)
        orders.append(jnp.sum(here, axis=0, keepdims=True))
        starts.append(jnp.sum(jnp.where(k < lane, 1, 0), axis=0, keepdims=True))
    return jnp.concatenate(orders + starts + [jnp.zeros((4, 128), jnp.int32)], axis=0)


def body(
    blocks_hbm, alpha_hbm, sbias_hbm, nbias_hbm, spos_hbm, npos_hbm, counts_hbm,
    rout_ref, cout_ref,
    blocks_ref, alpha_ref, sbias_ref, nbias_ref, spos_ref, npos_ref, counts_ref, in_sem,
    bvec_ref, table_ref, order_ref,
    s_ref, n_ref, nt_ref, st_ref, a_ref, racc, cacc, erow, ecol,
    ypiece, sib, xbuf, xin, zout, zin, lout, lin, yblk, yin,
    n_send, n_recv, f_send, f_recv, y_send, y_recv, z_send, z_recv,
    cf_send, cf_recv, cx_send, cx_recv, rz_send, rz_recv, l_send, l_recv, ry_send, ry_recv,
):
    x, core, y, z = position()
    xs, sibling, ys, zs = all_peers()
    width = npos_ref.shape[1]
    tiles = counts_ref.shape[0]
    copies = []

    def send(src, dst, ssem, rsem, peer):
        c = remote(src, dst, ssem, rsem, peer)
        c.start()
        copies.append(c)
        return c

    loads = [
        pltpu.make_async_copy(a, b, in_sem.at[i])
        for i, (a, b) in enumerate((
            (spos_hbm, spos_ref), (sbias_hbm, sbias_ref), (alpha_hbm, alpha_ref), (npos_hbm, npos_ref),
            (nbias_hbm, nbias_ref), (blocks_hbm, blocks_ref),
            (blocks_hbm, bvec_ref), (counts_hbm, counts_ref),
        ))
    ]
    for c in loads:
        c.start()
    corners = [
        {"row": lax.axis_index("row"), "col": (z + e) % NZ * NY + (y + d) % NY} for e in LATE for d in YD
    ]
    peers = [xs[d] for d in XD] + [sibling] + [ys[d] for d in YD] + [zs[d] for d in ZD] + corners
    greet(peers)

    for c in loads[0:3]:
        c.wait()
    sp = spos_ref[...].astype(F32)
    u = LOG2E * (alpha_ref[0, 0] + sbias_ref[...].astype(F32) - jnp.sum(sp * sp, axis=0, keepdims=True))
    ypiece[y] = jnp.zeros((KROWS, 128), BF16)
    ypiece[y, 0:64, 0:64] = spos_ref[...]
    ypiece[y, 64:80, 0:64] = extras(u)

    for c in loads[3:5]:
        c.wait()
    nodes = npos_ref[...].astype(F32)
    nb = nbias_ref[...].astype(F32)
    nb = jnp.concatenate([nb[i : i + 1] for i in range(width // 128)], axis=1)
    v = LOG2E * (nb - jnp.sum(nodes * nodes, axis=0, keepdims=True))
    mine = columns(n_ref, x * 2 + core, width)
    mine[0:64, :] = npos_ref[...]
    mine[64:80, :] = extras(v)
    pl.semaphore_wait(pltpu.get_barrier_semaphore(), len(peers))
    yget = {d: send(ypiece.at[y], ypiece.at[y], y_send.at[d], y_recv.at[d], ys[d]) for d in YD}
    for d in XNEAR:
        send(mine, mine, n_send.at[d], n_recv.at[d], xs[d])
    f0 = send(mine, mine, f_send.at[0], f_recv.at[0], sibling)

    def spans(n, f):
        def step(i, _):
            f(i)
            return 0

        lax.fori_loop(0, n, step, 0)

    for c in loads[5:8]:
        c.wait()

    racc[...] = jnp.zeros_like(racc)
    cacc[...] = jnp.zeros_like(cacc)
    table_ref[...] = jnp.zeros_like(table_ref)
    table_ref[0:2, 0:tiles] = bvec_ref[...]
    table_ref[...] = tile_tables(table_ref[...], tiles)
    tables = pltpu.make_async_copy(table_ref, order_ref, in_sem.at[8])
    tables.start()

    for d in YD:
        yget[d].wait_recv()
    lane = lax.broadcasted_iota(jnp.int32, (KROWS, 128), 1)
    own = s_ref.at[:, pl.ds(SLOT[0] * 256, 256)]
    for h in range(2):
        a, b = ypiece[2 * h].astype(F32), ypiece[2 * h + 1].astype(F32)
        own[:, h * 128 : h * 128 + 128] = jnp.where(lane < 64, a, pltpu.roll(b, 64, 1)).astype(BF16)
    zget = {}
    for d in ZSEND:
        dst = s_ref.at[:, pl.ds(SLOT[d] * 256, 256)]
        zget[d] = send(own, dst, z_send.at[d], z_recv.at[d], zs[d])

    def chip(d):
        return (x + d) % NX

    near, far = 1 + 2 * core, 3 - 2 * core

    def npiece(d, k):
        return columns(n_ref, chip(NX - d) * 2 + k, width)

    def npass(d):
        remote(npiece(d, core), npiece(d, core), n_send.at[d], n_recv.at[d], sibling).wait_recv()
        remote(npiece(d, core), npiece(d, core), f_send.at[d], f_recv.at[d], sibling).start()

    def prep_rows(slot):
        sl = pl.ds(slot * 256, 256)
        s = s_ref[:, sl].astype(F32)
        h1, h2, h3 = split3(s[0:64] * (2.0 * LOG2E))
        k = lax.broadcasted_iota(jnp.int32, (16, 256), 0)
        one = jnp.where((k >= 1) & (k <= 3), 1.0, 0.0)
        e = jnp.where(k == 0, s[65:66], jnp.where(k == 4, s[66:67], jnp.where(k == 5, s[67:68], one)))
        t = jnp.concatenate([h1, h2, h3, e, jnp.zeros((48, 256), F32)], axis=0)
        a_ref[sl, :] = t.astype(BF16).T

    def prep_cols(j):
        n = columns(n_ref, j, width)[...]
        t = jnp.concatenate([n, jnp.zeros((48, width), BF16)], axis=0).T
        nt_ref[pl.ds(j * (width // TB), width // TB)] = t.reshape(width // TB, TB, 128)

    def sweep(row, n_rows, column, n_cols):
        q = pl.ds(pl.multiple_of(column, 128), n_cols)
        sl = pl.ds(pl.multiple_of(row, 128), n_rows)
        n = n_ref[:, q]
        b = jnp.concatenate([n[0:64], n[0:64], n, jnp.zeros((48, n_cols), BF16)], axis=0)
        t = jnp.dot(a_ref[sl, :], b, preferred_element_type=F32)
        lam = jnp.exp2(t).astype(BF16)
        nt = nt_ref[pl.ds(column // TB, n_cols // TB)].reshape(n_cols, 128)
        racc[sl, :] -= jnp.dot(lam, nt, preferred_element_type=F32)
        cacc[:, q] -= jnp.dot(s_ref[:, sl], lam, preferred_element_type=F32)

    def pair(c):
        sweep(0, 512, c * (2 * width), 2 * width)

    def single(slot, c):
        sweep(slot * 256, 256, c * (2 * width), 2 * width)

    prep_rows(SLOT[0])
    f0.wait_recv()
    prep_cols(x * 2)
    prep_cols(x * 2 + 1)
    single(SLOT[0], x)
    remote(npiece(near, core), npiece(near, core), n_send.at[near], n_recv.at[near], sibling).wait_recv()
    onward = {"row": chip(near) * 2 + core, "col": lax.axis_index("col")}
    send(npiece(near, core), npiece(near, core), n_send.at[2], n_recv.at[2], onward)
    remote(npiece(near, core), npiece(near, core), f_send.at[near], f_recv.at[near], sibling).start()
    npass(far)


    def nready(d):
        remote(npiece(d, core), npiece(d, core), f_send.at[d], f_recv.at[d], sibling).wait_recv()

    def own_near(i):
        d = 1 + 2 * i
        nready(d)
        c = chip(NX - d)
        prep_cols(c * 2)
        prep_cols(c * 2 + 1)
        single(SLOT[0], c)

    spans(2, own_near)
    for d in ORDER[0:2]:
        zget[d].wait_recv()
        prep_rows(SLOT[d])
    pair(x)
    npass(2)
    spans(2, lambda i: pair(chip(3 + i * 2)))
    nready(2)
    for d in XD:
        copies.append(remote(npiece(d, core), npiece(d, core), f_send.at[d], f_recv.at[d], sibling))
    prep_cols(chip(2) * 2)
    prep_cols(chip(2) * 2 + 1)
    single(SLOT[0], chip(2))
    pair(chip(2))
    for d in ORDER[2:-1]:
        zget[d].wait_recv()
        prep_rows(SLOT[d])

    for d in ORDER:
        for h in range(2):
            st_ref[(z + NZ - d) % NZ * 2 + h] = s_ref[:, pl.ds(SLOT[d] * 256 + h * TB, TB)]
    tables.wait()
    erow[0] = jnp.zeros((TB, 128), F32)
    ecol[0] = jnp.zeros((KROWS, TB), F32)

    def entry(row, at, most):
        return jnp.minimum(jnp.maximum(order_ref[row, at], 0), most)

    def edge(g):
        rsum, csum = erow[g * 4], ecol[g * 4]
        for i in range(4):
            m = g * 4 + i
            k = entry(0, m, tiles - 1)
            yk = counts_ref[k].astype(F32).astype(BF16)
            rsum += jnp.dot(yk, nt_ref[blocks_ref[1, k]], preferred_element_type=F32)
            erow[m + 1] = rsum
            k = entry(1, m, tiles - 1)
            yk = counts_ref[k].astype(F32).astype(BF16)
            csum += jnp.dot(st_ref[blocks_ref[0, k]], yk, preferred_element_type=F32)
            ecol[m + 1] = csum

    spans(tiles // 4, edge)

    def place_cols(g):
        for i in range(4):
            t = g * 4 + i
            cacc[:, pl.ds(pl.multiple_of(t * TB, TB), TB)] += ecol[entry(3, t + 1, tiles)] - ecol[entry(3, t, tiles)]

    spans(cacc.shape[1] // TB // 4, place_cols)

    def centred(sums, pos):
        return jnp.concatenate([sums[0:64] - pos[0:64].astype(F32) * sums[64:65], sums[64:80]], axis=0)

    def rows_done(slot, d):
        parts = []
        for h in range(2):
            t = (z + NZ - d) % NZ * 2 + h
            acc = racc[pl.ds(pl.multiple_of(slot * 256 + h * TB, TB), TB), :]
            parts.append(acc + erow[entry(2, t + 1, tiles)] - erow[entry(2, t, tiles)])
        return centred(jnp.concatenate(parts, axis=0).T[0:KROWS], columns(s_ref, slot, 256)[...])

    rget = {}

    def rows_out(slot):
        e = (NZ - ORDER[slot]) % NZ
        zout[e] = rows_done(slot, ORDER[slot]).astype(BF16)
        rget[e] = send(zout.at[e], zin.at[e], rz_send.at[e], rz_recv.at[e], zs[e])

    def pack(block):
        lane = lax.broadcasted_iota(jnp.int32, (PIECE, 128), 1)
        out = []
        for h in range(2):
            top, low = block[0:PIECE, h * 128 : h * 128 + 128], block[PIECE:KROWS, h * 128 : h * 128 + 128]
            out.append(jnp.where(lane < 64, top, pltpu.roll(low, 64, 1)))
            out.append(jnp.where(lane < 64, pltpu.roll(top, 64, 1), low))
        return out

    def late_copy(i, t):
        e = NZ - (9 - 2 * i) % NZ
        peer = {"row": lax.axis_index("row"), "col": (z + e) % NZ * NY + (y + t) % NY}
        return remote(lout.at[i, (y + t) % NY], lin.at[i, t], l_send.at[i, t], l_recv.at[i, t], peer)

    def rows_late(i):
        for t, p in enumerate(pack(rows_done(4 + i, (9 - 2 * i) % NZ))):
            lout[i, t, 0:PIECE] = p.astype(BF16)
        for t in range(NY):
            late_copy(i, t).start()

    def core_copy(d):
        src = columns(cacc, chip(d) * 2 + 1 - core, width).at[0:OROWS]
        return remote(src, sib.at[d], cf_send.at[d], cf_recv.at[d], sibling)

    def cols_sum(d):
        core_copy(d).wait_recv()
        xbuf[d] = columns(cacc, chip(d) * 2 + core, width)[0:OROWS] + sib[d]

    def chip_copy(d):
        peer = {"row": chip(d) * 2 + core, "col": lax.axis_index("col")}
        return remote(xbuf.at[d], xin.at[d], cx_send.at[d], cx_recv.at[d], peer)

    def four(d, k):
        sweep(512, 1024, (chip(d) * 2 + k) * width, width)

    rows_out(0)
    rows_out(1)
    single(6, chip(2))
    def far_units(i):
        four(2, (1 + core + i) % 2)

        @pl.when(i == 0)
        def _():
            core_copy(2).start()

    spans(2, far_units)
    spans(3, lambda i: single(6, chip(3 + i)))
    rows_out(6)
    cols_sum(2)
    relayed = send(xbuf.at[2], xin.at[2], cx_send.at[2], cx_recv.at[2], onward)

    def near_units(i):
        d = 1 + i % 2 * 2
        sweep(1024, 512, (chip(d) * 2 + (1 + core + i // 2) % 2) * width, width)

        @pl.when(i < 2)
        def _():
            core_copy(d).start()

        @pl.when(i >= 2)
        def _():
            cols_sum(d)

            @pl.when(near == d)
            def _():
                relayed.wait_recv()
                xbuf[d] += xin[2]

            chip_copy(d).start()

    spans(3, lambda i: sweep(512, 512, chip(3 + i) * (2 * width), 2 * width))
    rows_out(2)
    rows_out(3)
    spans(4, near_units)

    def y_copy(d):
        return remote(yblk.at[(y + d) % NY], yin.at[d], ry_send.at[d], ry_recv.at[d], ys[d])

    def late_units(i):
        single(4 + i, x)

        @pl.when(i == 1)
        def _():
            core_copy(0).start()

        rows_late(i)

        @pl.when(i == 0)
        def _():
            total = rows_done(7, 0)
            for e in (6, 2, 4, 5, 3):
                rget[e].wait_recv()
                total += zin[e].astype(F32)
            for t, p in enumerate(pack(total)):
                yblk[t] = p
            for d in YD:
                y_copy(d).start()

    spans(2, late_units)

    for d in XNEAR:
        chip_copy(d).wait_recv()
        copies.append(chip_copy(d))
    core_copy(0).wait_recv()
    for d in range(NX):
        copies.append(core_copy(d))
    for h in range(width // 256):
        sl = pl.ds(h * 256, 256)
        acc = columns(cacc, x * 2 + core, width)[0:OROWS, sl] + sib[0, :, sl]
        acc += xin[1, :, sl] + xin[3, :, sl]
        cout_ref[:, sl] = acc

    own_sums = yblk[y]
    for i in range(len(LATE)):
        for t in range(NY):
            late_copy(i, t).wait_recv()
            copies.append(late_copy(i, t))
            own_sums += lin[i, t, 0:PIECE].astype(F32)
    for d in YD:
        y_copy(d).wait_recv()
        copies.append(y_copy(d))
        own_sums += yin[d]
    rout_ref[...] = own_sums
    for c in copies:
        c.wait_send()


def finish(npos_ref, rows_ref, cols_ref, sg_ref, sb_ref, ng_ref, nb_ref, *, n_nodes, n_slab):
    r = rows_ref[...]
    low = pltpu.roll(r, 64, 1)
    sums = jnp.concatenate([r, low], axis=0)[:, 0:64]
    sg_ref[...] = sums[0:64] * (2.0 / n_nodes)
    sb_ref[...] = sums[64:65] * (1.0 / n_nodes)
    tot = cols_ref[64:65, :]
    ng_ref[...] = (cols_ref[0:64, :] - npos_ref[...].astype(F32) * tot) * (2.0 / n_slab)
    nb_ref[...] = tot * (1.0 / n_slab)


def local(slab_pos, slab_bias, node_pos, node_bias, alpha, edge_counts, edge_blocks):
    vmem = pl.BlockSpec(memory_space=pltpu.VMEM)
    hbm = pl.BlockSpec(memory_space=pltpu.HBM)
    dma = pltpu.SemaphoreType.DMA
    own_rows, own_cols = slab_pos.shape[1], node_pos.shape[1]
    rows = own_rows * lax.axis_size("col")
    cols = own_cols * lax.axis_size("row")
    n_slab = rows * lax.axis_size("row")
    n_nodes = cols * lax.axis_size("col")
    tiles = edge_counts.shape[0]
    pieces = [pltpu.VMEM((NX, OROWS, own_cols), F32)] * 3
    group = pltpu.VMEM((NZ, KROWS, 256), BF16)
    row_sums, col_sums = pl.pallas_call(
        body,
        out_shape=(jax.ShapeDtypeStruct((PIECE, 128), F32), jax.ShapeDtypeStruct((OROWS, own_cols), F32)),
        in_specs=[hbm] * 7,
        out_specs=(vmem,) * 2,
        scratch_shapes=[
            pltpu.SMEM((2, tiles), jnp.int32), pltpu.SMEM((1, 1), F32), pltpu.VMEM((1, own_rows), BF16),
            pltpu.VMEM((own_cols // 128, 128), BF16), pltpu.VMEM(slab_pos.shape, BF16), pltpu.VMEM(node_pos.shape, BF16),
            pltpu.VMEM(edge_counts.shape, jnp.int32), dma((9,)),
            pltpu.VMEM((2, tiles), jnp.int32), pltpu.VMEM((8, 128), jnp.int32), pltpu.SMEM((8, 128), jnp.int32),
            pltpu.VMEM((KROWS, rows), BF16), pltpu.VMEM((KROWS, cols), BF16), pltpu.VMEM((cols // TB, TB, 128), BF16),
            pltpu.VMEM((rows // TB, KROWS, TB), BF16),
            pltpu.VMEM((rows, 256), BF16), pltpu.VMEM((rows, 128), F32), pltpu.VMEM((KROWS, cols), F32),
            pltpu.VMEM((tiles + 1, TB, 128), F32), pltpu.VMEM((tiles + 1, KROWS, TB), F32),
            pltpu.VMEM((NY, KROWS, 128), BF16), *pieces, group, group,
            pltpu.VMEM((len(LATE), NY, 48, 128), BF16), pltpu.VMEM((len(LATE), NY, 48, 128), BF16),
            pltpu.VMEM((NY, PIECE, 128), F32), pltpu.VMEM((NY, PIECE, 128), F32),
        ] + [dma((NX,))] * 4 + [dma((NY,))] * 2 + [dma((NZ,))] * 2
        + [dma((NX,))] * 4 + [dma((NZ,))] * 2 + [dma((len(LATE), NY))] * 2 + [dma((NY,))] * 2,
        compiler_params=params(collective_id=0, has_side_effects=True),
        name="gradient",
    )(
        edge_blocks.T, alpha.reshape(1, 1), slab_bias.reshape(1, own_rows), node_bias.reshape(own_cols // 128, 128),
        slab_pos, node_pos, edge_counts,
    )
    sg, sb, ng, nb = pl.pallas_call(
        functools.partial(finish, n_nodes=n_nodes, n_slab=n_slab),
        out_shape=(
            jax.ShapeDtypeStruct((64, own_rows), F32), jax.ShapeDtypeStruct((1, own_rows), F32),
            jax.ShapeDtypeStruct((64, own_cols), F32), jax.ShapeDtypeStruct((1, own_cols), F32),
        ),
        in_specs=[vmem] * 3,
        out_specs=(vmem,) * 4,
        compiler_params=params(),
        name="finish",
    )(node_pos, row_sums, col_sums)
    return sg, sb.reshape(own_rows), ng, nb.reshape(own_cols)


def solution(mesh):
    in_specs = (
        P(None, ("row", "col")),
        P(("row", "col")),
        P(None, ("col", "row")),
        P(("col", "row")),
        P(),
        P(("row", "col"), None, None),
        P(("row", "col"), None),
    )
    out_specs = (
        P(None, ("row", "col")),
        P(("row", "col")),
        P(None, ("col", "row")),
        P(("col", "row")),
    )
    return jax.shard_map(local, mesh=mesh, in_specs=in_specs, out_specs=out_specs, check_vma=False)
```
